256 devices in a mesh: grp: 8 (over z), sub: 32 (over x, y, core).
Axes of the slice: x: 4, y: 4, z: 8, core: 2. Of those that a mesh axis runs over, the one named last changes fastest.
Arguments:
- residual: float32 [16, 98304], P(None, 'sub'), may hold values from -6 to 6
- margin: int32 [32, 8], replicated, may hold values from 0 to 767, as said below
- aggregate: int32 [768], P('sub'), may hold values from 0 to 63
- local_factor: bfloat16 [32, 4096, 4096], P('sub', 'grp'), may hold values from -0.09375 to 0.09375
- coarse_factor: bfloat16 [8192, 8192], P('sub'), may hold values from -0.0625 to 0.0625
Outputs:
- preconditioned: float32 [16, 98304], P('grp', 'sub')
The draws below stay inside these ranges and needn't reach their ends.
Inputs may be any that keep to these rules, and one draw needn't show every extreme that they name: `margin`: for subdomain s, every entry names a block owned by another subdomain (block b is owned by subdomain b // 24); the entries of one row are distinct. Up to 8 entries of one row may name blocks of the same owner, and in every draw some row takes all of its entries from a single owner. `aggregate`: the counts of global blocks for each coarse block are whole numbers and may cross devices as int32.
All inputs are finite; a program needn't handle non-finite values.
Results may differ from the reference program's by a relative error of at most 0.0033.
Values sent between devices are 32-bit elements; how exact they have to be, the bound alone decides.
A program may use at most 64 MiB of HBM per device.

```python
import math
import jax
import jax.numpy as jnp
import numpy as np
from jax import lax

BLK = 128
SUBB = 32
HALO = 8
NCB = 64
NRHS = 16
OWN = 24
SUBN = 4096
NC = 8192
NFB = 768
NCELL = 98304
N_SUB = 32


def draw_margin(key, part):
    base = jax.random.fold_in(key, 11)
    first_key, second_key, third_key, fourth_key, fifth_key = jax.random.split(base, 5)
    distance = jax.random.randint(first_key, (N_SUB, HALO), 1, N_SUB)
    far_slot = jax.random.randint(third_key, (N_SUB, 1), 0, HALO)
    slot_ids = jnp.arange(HALO, dtype=jnp.int32)[None, :]
    distance = jnp.where(slot_ids == far_slot, N_SUB // 2, distance)
    full_row = jax.random.randint(fourth_key, (), 0, N_SUB)
    full_distance = jax.random.randint(fifth_key, (), 1, N_SUB)
    row_ids = jnp.arange(N_SUB, dtype=jnp.int32)[:, None]
    distance = jnp.where(row_ids == full_row, full_distance, distance)
    owners = (jnp.arange(N_SUB, dtype=jnp.int32)[:, None] + distance) % N_SUB
    subkeys = jax.random.split(second_key, N_SUB)

    def slot_row(row_key):
        return jax.random.permutation(row_key, OWN)[:HALO]
    in_slot = jax.vmap(slot_row)(subkeys)
    return (owners * OWN + in_slot).astype(jnp.int32)


def with_ends(drawn, own_key, low, high):
    longest = drawn.shape.index(max(drawn.shape))
    spots = []
    for shift in (0, 1):
        where = [jax.random.randint(jax.random.fold_in(own_key, axis), (), 0, length) for axis, length in enumerate(drawn.shape)]
        where[longest] = (where[longest] + shift) % drawn.shape[longest]
        spots.append(tuple(where))
    return drawn.at[spots[0]].set(low).at[spots[1]].set(high)


def level_of(rng, extent, shards, low, top_value):
    level, own = 1.0, jax.random.fold_in(rng, 6)
    for axis_at, shards_of in shards:
        heights = jnp.exp(jax.random.uniform(jax.random.fold_in(own, axis_at), (shards_of,), jnp.float32, low / len(shards), top_value / len(shards)))
        level = level * jnp.repeat(heights, extent[axis_at] // shards_of).reshape([-1 if axis == axis_at else 1 for axis in range(len(extent))])
    return level


def rank_table(count, slope):
    weights = [(1 << 20) // math.isqrt(grade ** slope) + 1 for grade in range(1, count + 1)]
    width = 1 + sum(weights) // (1 << 30)
    return np.cumsum(np.array([max(1, weight // width) for weight in weights]))


def ranked_ids(key, shape, number_of, slope):
    listing = rank_table(number_of, slope)
    pick = jax.random.randint(jax.random.fold_in(key, 1), shape, 0, int(listing[number_of - 1]))
    standing = jnp.searchsorted(jnp.asarray(listing, jnp.int32), pick, side="right")
    return jax.random.permutation(jax.random.fold_in(key, 2), number_of)[standing].astype(jnp.int32)


def noise(stream_key, dims, width, limit, cuts=(), kind=jnp.bfloat16):
    array = jax.random.normal(stream_key, dims, jnp.float32) * width
    if len(cuts) > 0:
        array = level_of(stream_key, dims, cuts, -0.22, 0.18) * array
    return jnp.clip(array, min=-limit, max=limit).astype(kind)


def setup_inputs(seed: int = 0) -> dict:
    key_of = jax.random.split(jax.random.key(seed), 6)
    return {
        "residual": noise(key_of[0], (NRHS, NCELL), 1.0, 6.0, ((1, 32),), jnp.float32),
        "margin": draw_margin(jax.random.fold_in(key_of[5], 71), 0),
        "aggregate": with_ends(ranked_ids(key_of[2], (NFB,), NCB, 2), jax.random.fold_in(key_of[2], 3), 0, NCB - 1).astype(jnp.int32),
        "local_factor": noise(key_of[3], (N_SUB, SUBN, SUBN), SUBN ** -0.5, 0.09375, ((0, 32), (1, 8))),
        "coarse_factor": noise(key_of[4], (NC, NC), NC ** -0.5, 0.0625, ((0, 32),)),
    }


def reference(residual, margin, aggregate, local_factor, coarse_factor):
    blocks = residual.reshape(NRHS, NFB, BLK)
    own_ids = jnp.arange(NFB, dtype=jnp.int32).reshape(N_SUB, OWN)
    block_ids = jnp.concatenate([own_ids, margin.astype(jnp.int32)], axis=1)

    def subdomain(summed, pieces):
        chosen, factor = pieces
        local_rhs = blocks[:, chosen, :].reshape(NRHS, SUBN).astype(jnp.bfloat16)
        inner_term = jnp.dot(local_rhs, factor.T, preferred_element_type=jnp.float32).astype(jnp.bfloat16)
        local_sol = jnp.dot(inner_term, factor, preferred_element_type=jnp.float32)
        summed = summed.at[:, chosen, :].add(local_sol.reshape(NRHS, SUBB, BLK))
        return summed, None

    summed, _ = lax.scan(subdomain, jnp.zeros((NRHS, NFB, BLK), jnp.float32), (block_ids, local_factor))
    catalog = jnp.arange(NCB, dtype=jnp.int32)
    member = (aggregate[:, None] == catalog[None, :]).astype(jnp.float32)
    sums = jnp.einsum('rbk,bj->rjk', blocks, member, precision=lax.Precision.HIGHEST)
    counts = jnp.sum(member, axis=0)
    coarse_rhs = (sums / jnp.maximum(counts, 1.0)[None, :, None]).reshape(NRHS, NC).astype(jnp.bfloat16)
    inner_coarse = jnp.dot(coarse_rhs, coarse_factor.T, preferred_element_type=jnp.float32).astype(jnp.bfloat16)
    coarse_sol = jnp.dot(inner_coarse, coarse_factor, preferred_element_type=jnp.float32)
    prolonged = jnp.einsum('rjk,bj->rbk', coarse_sol.reshape(NRHS, NCB, BLK), member, precision=lax.Precision.HIGHEST)
    return (summed + prolonged).reshape(NRHS, NCELL)
```

```python
import functools

import jax
import jax.numpy as jnp
from jax import lax
from jax.experimental import pallas as pl
from jax.experimental.pallas import tpu as pltpu
from jax.sharding import PartitionSpec as P

BLK = 128
F32 = jnp.float32
BF16 = jnp.bfloat16
MESH = pl.DeviceIdType.MESH
NT = (((1,), (1,)), ((), ()))


def split_dot(onehot, values):
    high = values.astype(BF16)
    low = (values - high.astype(F32)).astype(BF16)
    return jnp.dot(onehot, high, preferred_element_type=F32) + jnp.dot(
        onehot, low, preferred_element_type=F32
    )


def wait_all(ref, sem):
    pltpu.make_async_copy(ref, ref, sem).wait()


def kernel(
    sizes,
    margin, aggregate, residual, local_factor, coarse_factor,
    out,
    res_v, w_v, v_v, gathered, pick_out, pick_in, sums_out, sums_in, halo, c_rows,
    part_h, recv_h, part_o, recv_o, back, e_part, e_recv, e_full, acc,
    load_sem, gather_send, gather_recv, pair_send, pair_recv, halo_send, halo_recv,
    h_send, h_recv, o_send, o_recv, back_send, back_recv, es_send, es_recv, ea_send, ea_recv,
):
    n_sub, n_grp, own, margins, ncb = sizes
    nq = n_sub // 2
    rows = 2
    per = ncb // n_sub
    me = lax.axis_index("sub")
    grp = lax.axis_index("grp")
    core = lax.rem(me, 2)
    q = lax.div(me, 2)
    pair = me + 1 - 2 * core

    for b in range(own):
        pltpu.make_async_copy(
            residual.at[:, pl.ds(b * BLK, BLK)], res_v.at[b], load_sem.at[0]
        ).start()
    load_w = pltpu.make_async_copy(local_factor.at[0], w_v, load_sem.at[1])
    load_v = pltpu.make_async_copy(coarse_factor, v_v, load_sem.at[2])
    load_w.start()
    load_v.start()

    barrier = pltpu.get_barrier_semaphore()

    def greet_plane(d, carry):
        pl.semaphore_signal(
            barrier, inc=1, device_id=(grp, lax.rem(me + d, n_sub)), device_id_type=MESH
        )
        return carry

    def greet_column(d, carry):
        pl.semaphore_signal(
            barrier, inc=1, device_id=(lax.rem(grp + d, n_grp), me), device_id_type=MESH
        )
        return carry

    lax.fori_loop(1, n_sub, greet_plane, 0)
    lax.fori_loop(1, n_grp, greet_column, 0)

    place = (
        lax.broadcasted_iota(jnp.int32, (8, BLK), 0) * BLK
        + lax.broadcasted_iota(jnp.int32, (8, BLK), 1)
    )
    mark = jnp.zeros((8, BLK), F32)
    for b in range(own):
        mark = jnp.where(place == q * own + b, (aggregate[b] + 1).astype(F32), mark)
    wait_all(res_v, load_sem.at[0])
    for r in range(rows):
        for b in range(own):
            gathered[q, r * own + b : r * own + b + 1, :] = res_v[
                b, pl.ds(grp * rows + r, 1), :
            ]
    gathered[q, rows * own : rows * own + 8, :] = mark
    pl.semaphore_wait(barrier, n_sub - 1 + n_grp - 1)

    def send_gather(d, carry):
        target = lax.rem(q + d, nq) * 2 + core
        pltpu.make_async_remote_copy(
            src_ref=gathered.at[q], dst_ref=gathered.at[q],
            send_sem=gather_send, recv_sem=gather_recv,
            device_id=(grp, target), device_id_type=MESH,
        ).start()
        return carry

    lax.fori_loop(1, nq, send_gather, 0)

    load_w.wait()
    width = own * BLK
    inner = lax.dot_general(
        jnp.concatenate([res_v[b].astype(BF16) for b in range(own)], axis=1),
        w_v[:, :width], NT, preferred_element_type=F32,
    )
    table_rows = -(-n_sub * margins // BLK)

    def fill_table(s, table):
        for k in range(margins):
            table = jnp.where(place == s * margins + k, margin[s, k], table)
        return table

    table = lax.fori_loop(0, n_sub, fill_table, jnp.full((8, BLK), -1, jnp.int32))
    own_ids = lax.broadcasted_iota(jnp.int32, (own, BLK), 0) + me * own
    owner_hot = jnp.concatenate(
        [
            (jnp.broadcast_to(table[i : i + 1, :], (own, BLK)) == own_ids).astype(F32)
            for i in range(table_rows)
        ],
        axis=1,
    ).astype(BF16)

    wait_all(gathered.at[pl.ds(0, nq - 1)], gather_recv)

    def pick(sub_index, target):
        for k in range(margins):
            block = margin[sub_index, k]
            owner = lax.div(block, own)
            slot = lax.div(owner, 2)
            at = block - owner * own
            for r in range(rows):
                target[r : r + 1, k * BLK : (k + 1) * BLK] = gathered[
                    slot, pl.ds(at + r * own, 1), :
                ]

    pick(pair, pick_out)
    pair_pick = pltpu.make_async_remote_copy(
        src_ref=pick_out, dst_ref=pick_in, send_sem=pair_send.at[0], recv_sem=pair_recv.at[0],
        device_id=(grp, pair), device_id_type=MESH,
    )
    pair_pick.start()
    pick(me, halo.at[grp])

    marks = gathered[0, rows * own : rows * own + 8, :]
    for i in range(1, nq):
        marks = marks + gathered[i, rows * own : rows * own + 8, :]
    depth = nq * own
    tiles = -(-depth // BLK)
    coarse_ids = (lax.broadcasted_iota(jnp.int32, (ncb, BLK), 0) + 1).astype(F32)

    def hot_of(m):
        return jnp.concatenate(
            [
                (jnp.broadcast_to(m[i : i + 1, :], (ncb, BLK)) == coarse_ids).astype(F32)
                for i in range(tiles)
            ],
            axis=1,
        )

    hot = hot_of(marks)
    values = jnp.concatenate(
        [gathered[:, r * own : (r + 1) * own, :].reshape(depth, BLK) for r in range(rows)], axis=1
    )
    part_sums = split_dot(hot[:, :depth].astype(BF16), values)
    sums_out[:ncb, :] = part_sums
    sums_out[ncb:, :BLK] = marks
    sums_out[ncb:, BLK:] = marks
    pair_sums = pltpu.make_async_remote_copy(
        src_ref=sums_out, dst_ref=sums_in, send_sem=pair_send.at[1], recv_sem=pair_recv.at[1],
        device_id=(grp, pair), device_id_type=MESH,
    )
    pair_sums.start()

    pair_pick.wait_recv()
    for k in range(margins):
        owner = lax.div(margin[me, k], own)
        mine = lax.rem(owner, 2) == core
        cols = slice(k * BLK, (k + 1) * BLK)
        halo[grp, :, cols] = jnp.where(mine, halo[grp, :, cols], pick_in[:, cols])

    def column_copy(src, dst, send, recv, d):
        target = lax.rem(grp + d, n_grp)
        return pltpu.make_async_remote_copy(
            src_ref=src(target), dst_ref=dst.at[grp], send_sem=send, recv_sem=recv,
            device_id=(target, me), device_id_type=MESH,
        )

    def send_halo(d, carry):
        column_copy(lambda t: halo.at[grp], halo, halo_send, halo_recv, d).start()
        return carry

    lax.fori_loop(1, n_grp, send_halo, 0)

    pair_sums.wait_recv()
    count = jnp.sum(hot, axis=1, keepdims=True) + jnp.sum(
        hot_of(sums_in[ncb:, :BLK]), axis=1, keepdims=True
    )
    coarse = (part_sums + sums_in[:ncb, :]) / jnp.maximum(count, 1.0)
    for j in range(ncb):
        for r in range(rows):
            c_rows[r : r + 1, j * BLK : (j + 1) * BLK] = coarse[
                j : j + 1, r * BLK : (r + 1) * BLK
            ]
    load_v.wait()
    inner_c = lax.dot_general(
        c_rows[...].astype(BF16), v_v[...], NT, preferred_element_type=F32
    ).astype(BF16)
    e_mine = jnp.dot(inner_c, v_v[...], preferred_element_type=F32)
    for j in range(ncb):
        e_part[j] = e_mine[:, j * BLK : (j + 1) * BLK]

    def send_e_part(d, carry):
        target = lax.rem(me + d, n_sub)
        pltpu.make_async_remote_copy(
            src_ref=e_part.at[pl.ds(target * per, per)], dst_ref=e_recv.at[me],
            send_sem=es_send, recv_sem=es_recv,
            device_id=(grp, target), device_id_type=MESH,
        ).start()
        return carry

    lax.fori_loop(1, n_sub, send_e_part, 0)

    wait_all(halo.at[pl.ds(0, n_grp - 1)], halo_recv)
    halo_rhs = jnp.concatenate([halo[i] for i in range(n_grp)], axis=0).astype(BF16)
    inner = inner + lax.dot_general(
        halo_rhs, w_v[:, width:], NT, preferred_element_type=F32
    )
    inner = inner.astype(BF16)
    sol = jnp.dot(inner, w_v[:, width:], preferred_element_type=F32)
    for i in range(n_grp):
        part_h[i] = sol[i * rows : (i + 1) * rows, :]

    def send_h(d, carry):
        column_copy(lambda t: part_h.at[t], recv_h, h_send, h_recv, d).start()
        return carry

    lax.fori_loop(1, n_grp, send_h, 0)
    sol = jnp.dot(inner, w_v[:, :width], preferred_element_type=F32)
    for i in range(n_grp):
        part_o[i] = sol[i * rows : (i + 1) * rows, :]

    def send_o(d, carry):
        column_copy(lambda t: part_o.at[t], recv_o, o_send, o_recv, d).start()
        return carry

    lax.fori_loop(1, n_grp, send_o, 0)

    wait_all(e_recv.at[pl.ds(0, n_sub - 1)], es_recv)
    e_recv[me] = e_part[pl.ds(me * per, per)]
    e_full[pl.ds(me * per, per)] = jnp.sum(e_recv[...], axis=0)

    def send_e(d, carry):
        target = lax.rem(me + d, n_sub)
        pltpu.make_async_remote_copy(
            src_ref=e_full.at[pl.ds(me * per, per)], dst_ref=e_full.at[pl.ds(me * per, per)],
            send_sem=ea_send, recv_sem=ea_recv,
            device_id=(grp, target), device_id_type=MESH,
        ).start()
        return carry

    lax.fori_loop(1, n_sub, send_e, 0)

    wait_all(recv_h.at[pl.ds(0, n_grp - 1)], h_recv)
    recv_h[grp] = part_h[grp]
    total = jnp.sum(recv_h[...], axis=0)
    for k in range(margins):
        for r in range(rows):
            back[me, k : k + 1, r * BLK : (r + 1) * BLK] = total[
                r : r + 1, k * BLK : (k + 1) * BLK
            ]

    def send_back(d, carry):
        target = lax.rem(me + d, n_sub)
        pltpu.make_async_remote_copy(
            src_ref=back.at[me], dst_ref=back.at[me], send_sem=back_send, recv_sem=back_recv,
            device_id=(grp, target), device_id_type=MESH,
        ).start()
        return carry

    lax.fori_loop(1, n_sub, send_back, 0)

    wait_all(recv_o.at[pl.ds(0, n_grp - 1)], o_recv)
    recv_o[grp] = part_o[grp]
    total = jnp.sum(recv_o[...], axis=0)
    wait_all(e_full.at[pl.ds(0, ncb - per)], ea_recv)
    for b in range(own):
        both = e_full[aggregate[b]] + total[:, b * BLK : (b + 1) * BLK]
        for r in range(rows):
            acc[r, b : b + 1, :] = both[r : r + 1, :]

    wait_all(back.at[pl.ds(0, n_sub - 1)], back_recv)
    returned = split_dot(owner_hot[:, : n_sub * margins], back[...].reshape(n_sub * margins, rows * BLK))
    for r in range(rows):
        out[r] = acc[r] + returned[:, r * BLK : (r + 1) * BLK]

    wait_all(gathered.at[pl.ds(0, nq - 1)], gather_send)
    pair_pick.wait_send()
    pair_sums.wait_send()
    wait_all(halo.at[pl.ds(0, n_grp - 1)], halo_send)
    wait_all(recv_h.at[pl.ds(0, n_grp - 1)], h_send)
    wait_all(recv_o.at[pl.ds(0, n_grp - 1)], o_send)
    wait_all(e_recv.at[pl.ds(0, n_sub - 1)], es_send)
    wait_all(e_full.at[pl.ds(0, ncb - per)], ea_send)
    wait_all(back.at[pl.ds(0, n_sub - 1)], back_send)


def on_device(residual, margin, aggregate, local_factor, coarse_factor):
    n_sub = lax.axis_size("sub")
    n_grp = lax.axis_size("grp")
    rhs, own_width = residual.shape
    own = own_width // BLK
    margins = margin.shape[1]
    inner = local_factor.shape[1]
    nc = coarse_factor.shape[1]
    ncb = nc // BLK
    rows = rhs // n_grp
    nq = n_sub // 2
    hw = margins * BLK
    sizes = (n_sub, n_grp, own, margins, ncb)
    vm = pltpu.VMEM
    sem = pltpu.SemaphoreType.DMA
    result = pl.pallas_call(
        functools.partial(kernel, sizes),
        out_shape=jax.ShapeDtypeStruct((rows, own, BLK), F32),
        in_specs=[
            pl.BlockSpec(memory_space=pltpu.SMEM),
            pl.BlockSpec(memory_space=pltpu.SMEM),
            pl.BlockSpec(memory_space=pl.ANY),
            pl.BlockSpec(memory_space=pl.ANY),
            pl.BlockSpec(memory_space=pl.ANY),
        ],
        out_specs=pl.BlockSpec(memory_space=pltpu.VMEM),
        scratch_shapes=[
            vm((own, rhs, BLK), F32),
            vm((inner, own_width + hw), BF16),
            vm(coarse_factor.shape, BF16),
            vm((nq, rows * own + 8, BLK), F32),
            vm((rows, hw), F32),
            vm((rows, hw), F32),
            vm((ncb + 8, rows * BLK), F32),
            vm((ncb + 8, rows * BLK), F32),
            vm((n_grp, rows, hw), F32),
            vm((rows, nc), F32),
            vm((n_grp, rows, hw), F32),
            vm((n_grp, rows, hw), F32),
            vm((n_grp, rows, own_width), F32),
            vm((n_grp, rows, own_width), F32),
            vm((n_sub, margins, rows * BLK), F32),
            vm((ncb, rows, BLK), F32),
            vm((n_sub, ncb // n_sub, rows, BLK), F32),
            vm((ncb, rows, BLK), F32),
            vm((rows, own, BLK), F32),
            sem((3,)), sem, sem, sem((2,)), sem((2,)), sem, sem,
            sem, sem, sem, sem, sem, sem, sem, sem, sem, sem,
        ],
        compiler_params=pltpu.CompilerParams(collective_id=0, has_side_effects=True),
    )(margin, aggregate, residual, local_factor, coarse_factor)
    return result.reshape(rows, own_width)


def solution(mesh):
    placed = (P(None, "sub"), P(), P("sub"), P("sub", "grp", None), P("sub", None))
    return jax.shard_map(
        on_device, mesh=mesh, in_specs=placed, out_specs=P("grp", "sub"), check_vma=False
    )
```

```python
import functools

import jax
import jax.numpy as jnp
from jax import lax
from jax.experimental import pallas as pl
from jax.experimental.pallas import tpu as pltpu
from jax.sharding import PartitionSpec as P

BLK = 128
F32 = jnp.float32
BF16 = jnp.bfloat16
MESH = pl.DeviceIdType.MESH
NT = (((1,), (1,)), ((), ()))
TN = (((0,), (0,)), ((), ()))


def split(values):
    high = values.astype(BF16)
    return high, (values - high.astype(F32)).astype(BF16)


def split_dot(onehot, values):
    high, low = split(values)
    return jnp.dot(onehot, high, preferred_element_type=F32) + jnp.dot(
        onehot, low, preferred_element_type=F32
    )


def wait_all(ref, sem):
    pltpu.make_async_copy(ref, ref, sem).wait()


def kernel(
    sizes,
    margin, aggregate, residual, local_factor, coarse_factor,
    out,
    res_v, w_v, v_v, mine, pick_out, pick_in, c_out, c_in, c_full, halo, inner_v,
    part_h, recv_h, part_o, recv_o, back, e_part, e_recv, e_full, acc,
    load_sem, pick_send, pick_recv, cs_send, cs_recv, ca_send, ca_recv, halo_send, halo_recv,
    h_send, h_recv, o_send, o_recv, back_send, back_recv, es_send, es_recv, ea_send, ea_recv,
):
    n_sub, n_grp, own, margins, ncb = sizes
    rows = 2
    per = ncb // n_sub
    me = lax.axis_index("sub")
    grp = lax.axis_index("grp")

    for b in range(own):
        pltpu.make_async_copy(
            residual.at[:, pl.ds(b * BLK, BLK)],
            res_v.at[pl.ds(b * rows * n_grp, rows * n_grp)],
            load_sem.at[0],
        ).start()
    load_w = pltpu.make_async_copy(local_factor.at[0], w_v, load_sem.at[1])
    load_v = pltpu.make_async_copy(coarse_factor, v_v, load_sem.at[2])
    load_w.start()
    load_v.start()

    barrier = pltpu.get_barrier_semaphore()

    def plane(d):
        return (grp, lax.rem(me + d, n_sub))

    def column(d):
        return (lax.rem(grp + d, n_grp), me)

    for d in range(1, n_sub):
        pl.semaphore_signal(barrier, inc=1, device_id=plane(d), device_id_type=MESH)
    for d in range(1, n_grp):
        pl.semaphore_signal(barrier, inc=1, device_id=column(d), device_id_type=MESH)

    def to_plane(src, dst, send, recv):
        for d in range(1, n_sub):
            target = plane(d)
            pltpu.make_async_remote_copy(
                src_ref=src(target[1]), dst_ref=dst, send_sem=send, recv_sem=recv,
                device_id=target, device_id_type=MESH,
            ).start()

    def to_column(src, dst, send, recv):
        for d in range(1, n_grp):
            target = column(d)
            pltpu.make_async_remote_copy(
                src_ref=src(target[0]), dst_ref=dst, send_sem=send, recv_sem=recv,
                device_id=target, device_id_type=MESH,
            ).start()

    place = (
        lax.broadcasted_iota(jnp.int32, (8, BLK), 0) * BLK
        + lax.broadcasted_iota(jnp.int32, (8, BLK), 1)
    )
    slots = n_sub * margins

    def fill_table(s, table):
        for k in range(margins):
            table = jnp.where(place == s * margins + k, margin[k, s], table)
        return table

    table = lax.fori_loop(0, n_sub, fill_table, jnp.full((8, BLK), -1, jnp.int32))
    own_ids = lax.broadcasted_iota(jnp.int32, (own, BLK), 0) + me * own
    owner_hot = jnp.concatenate(
        [
            (jnp.broadcast_to(table[i : i + 1, :], (own, BLK)) == own_ids).astype(F32)
            for i in range(-(-slots // BLK))
        ],
        axis=1,
    )[:, :slots]
    mark = jnp.full((8, BLK), -1, jnp.int32)
    for b in range(own):
        mark = jnp.where(place == b, aggregate[b], mark)
    coarse_hot = (
        jnp.broadcast_to(mark[0:1, :], (ncb, BLK))
        == lax.broadcasted_iota(jnp.int32, (ncb, BLK), 0)
    ).astype(F32)

    wait_all(res_v, load_sem.at[0])
    for b in range(own):
        for r in range(rows):
            mine[r * own + b : r * own + b + 1, :] = res_v[
                pl.ds(b * rows * n_grp + grp * rows + r, 1), :
            ]
    blocks = jnp.concatenate([mine[r * own : (r + 1) * own, :] for r in range(rows)], axis=1)
    high, low = split(blocks)
    picked = lax.dot_general(owner_hot.astype(BF16), high, TN, preferred_element_type=F32)
    for r in range(rows):
        pick_out[:, r * margins : (r + 1) * margins, :] = picked[
            :, r * BLK : (r + 1) * BLK
        ].reshape(n_sub, margins, BLK)
    hot = coarse_hot[:, :own].astype(BF16)
    sums = jnp.dot(hot, high, preferred_element_type=F32) + jnp.dot(
        hot, low, preferred_element_type=F32
    )
    count = jnp.broadcast_to(jnp.sum(coarse_hot, axis=1, keepdims=True), (ncb, BLK))
    sums = jnp.concatenate([sums, count], axis=1)
    for t in range(n_sub):
        c_out[t] = sums[t * per : (t + 1) * per, :]

    pl.semaphore_wait(barrier, n_sub - 1 + n_grp - 1)
    to_plane(lambda t: pick_out.at[t], pick_in.at[me], pick_send, pick_recv)
    to_plane(lambda t: c_out.at[t], c_in.at[me], cs_send, cs_recv)

    load_w.wait()
    width = own * BLK
    deep = rows * n_grp
    inner = lax.dot_general(
        jnp.concatenate(
            [res_v[b * deep : (b + 1) * deep, :].astype(BF16) for b in range(own)], axis=1
        ),
        w_v[:, :width], NT, preferred_element_type=F32,
    )
    inner_tiles = inner.shape[1] // BLK
    for i in range(inner_tiles):
        inner_v[i * deep : (i + 1) * deep, :] = inner[:, i * BLK : (i + 1) * BLK]

    wait_all(pick_in.at[pl.ds(0, n_sub - 1)], pick_recv)
    hr = rows * margins
    pick_in[me] = jnp.zeros((hr, BLK), F32)
    halo[pl.ds(grp * hr, hr)] = jnp.sum(pick_in[...], axis=0)
    mine_halo = halo.at[pl.ds(grp * hr, hr)]
    to_column(lambda t: mine_halo, mine_halo, halo_send, halo_recv)

    wait_all(c_in.at[pl.ds(0, n_sub - 1)], cs_recv)
    c_in[me] = c_out[me]
    sums = jnp.sum(c_in[...], axis=0)
    coarse = sums[:, : rows * BLK] / jnp.maximum(
        jnp.concatenate([sums[:, rows * BLK :]] * rows, axis=1), 1.0
    )
    for i in range(per):
        for r in range(rows):
            c_full[me * per + i, r : r + 1, :] = coarse[i : i + 1, r * BLK : (r + 1) * BLK]
    mine_c = c_full.at[pl.ds(me * per, per)]
    to_plane(lambda t: mine_c, mine_c, ca_send, ca_recv)

    wait_all(halo.at[pl.ds(0, (n_grp - 1) * hr)], halo_recv)
    halo_rhs = jnp.concatenate(
        [
            jnp.concatenate(
                [
                    halo[pl.ds(r * margins + k, n_grp, stride=hr), :]
                    for k in range(margins)
                ],
                axis=1,
            )
            for r in range(rows)
        ],
        axis=0,
    ).astype(BF16)
    inner = jnp.concatenate(
        [
            jnp.concatenate(
                [
                    inner_v[pl.ds(i * deep + r, n_grp, stride=rows), :]
                    for i in range(inner_tiles)
                ],
                axis=1,
            )
            for r in range(rows)
        ],
        axis=0,
    )
    inner = inner + lax.dot_general(halo_rhs, w_v[:, width:], NT, preferred_element_type=F32)
    inner = inner.astype(BF16)

    def scatter_rows(sol, dst, blocks_each):
        for r in range(rows):
            for k in range(blocks_each):
                dst[pl.ds(r * blocks_each + k, n_grp, stride=rows * blocks_each), :] = sol[
                    r * n_grp : (r + 1) * n_grp, k * BLK : (k + 1) * BLK
                ]

    scatter_rows(jnp.dot(inner, w_v[:, width:], preferred_element_type=F32), part_h, margins)
    to_column(
        lambda t: part_h.at[pl.ds(t * hr, hr)], recv_h.at[pl.ds(grp * hr, hr)], h_send, h_recv
    )

    wait_all(c_full.at[pl.ds(0, ncb - per)], ca_recv)
    load_v.wait()
    c_rows = jnp.concatenate([c_full[j] for j in range(ncb)], axis=1).astype(BF16)
    inner_c = lax.dot_general(c_rows, v_v[...], NT, preferred_element_type=F32).astype(BF16)
    e_mine = jnp.dot(inner_c, v_v[...], preferred_element_type=F32)
    for j in range(ncb):
        e_part[j] = e_mine[:, j * BLK : (j + 1) * BLK]
    to_plane(lambda t: e_part.at[pl.ds(t * per, per)], e_recv.at[me], es_send, es_recv)

    scatter_rows(jnp.dot(inner, w_v[:, :width], preferred_element_type=F32), part_o, own)
    orr = rows * own
    to_column(
        lambda t: part_o.at[pl.ds(t * orr, orr)], recv_o.at[pl.ds(grp * orr, orr)], o_send, o_recv
    )

    wait_all(recv_h.at[pl.ds(0, (n_grp - 1) * hr)], h_recv)
    recv_h[pl.ds(grp * hr, hr)] = part_h[pl.ds(grp * hr, hr)]
    back[me] = jnp.sum(recv_h[...].reshape(n_grp, hr, BLK), axis=0)
    to_plane(lambda t: back.at[me], back.at[me], back_send, back_recv)

    wait_all(e_recv.at[pl.ds(0, n_sub - 1)], es_recv)
    e_recv[me] = e_part[pl.ds(me * per, per)]
    e_full[pl.ds(me * per, per)] = jnp.sum(e_recv[...], axis=0)
    mine_e = e_full.at[pl.ds(me * per, per)]
    to_plane(lambda t: mine_e, mine_e, ea_send, ea_recv)

    wait_all(recv_o.at[pl.ds(0, (n_grp - 1) * orr)], o_recv)
    recv_o[pl.ds(grp * orr, orr)] = part_o[pl.ds(grp * orr, orr)]
    total = jnp.sum(recv_o[...].reshape(n_grp, orr, BLK), axis=0)
    wait_all(e_full.at[pl.ds(0, ncb - per)], ea_recv)
    for b in range(own):
        acc[b * rows : (b + 1) * rows, :] = e_full[aggregate[b]]
    for r in range(rows):
        acc[pl.ds(r, own, stride=rows), :] = (
            acc[pl.ds(r, own, stride=rows), :] + total[r * own : (r + 1) * own, :]
        )

    wait_all(back.at[pl.ds(0, n_sub - 1)], back_recv)
    values = jnp.concatenate(
        [
            back[:, r * margins : (r + 1) * margins, :].reshape(slots, BLK)
            for r in range(rows)
        ],
        axis=1,
    )
    returned = split_dot(owner_hot.astype(BF16), values)
    for r in range(rows):
        out[pl.ds(r, own, stride=rows), :] = (
            acc[pl.ds(r, own, stride=rows), :] + returned[:, r * BLK : (r + 1) * BLK]
        )

    wait_all(pick_in.at[pl.ds(0, n_sub - 1)], pick_send)
    wait_all(c_in.at[pl.ds(0, n_sub - 1)], cs_send)
    wait_all(halo.at[pl.ds(0, (n_grp - 1) * hr)], halo_send)
    wait_all(c_full.at[pl.ds(0, ncb - per)], ca_send)
    wait_all(recv_h.at[pl.ds(0, (n_grp - 1) * hr)], h_send)
    wait_all(recv_o.at[pl.ds(0, (n_grp - 1) * orr)], o_send)
    wait_all(e_recv.at[pl.ds(0, n_sub - 1)], es_send)
    wait_all(e_full.at[pl.ds(0, ncb - per)], ea_send)
    wait_all(back.at[pl.ds(0, n_sub - 1)], back_send)


def on_device(residual, margin, aggregate, local_factor, coarse_factor):
    n_sub = lax.axis_size("sub")
    n_grp = lax.axis_size("grp")
    rhs, own_width = residual.shape
    own = own_width // BLK
    margins = margin.shape[1]
    inner = local_factor.shape[1]
    ncb = coarse_factor.shape[1] // BLK
    rows = rhs // n_grp
    per = ncb // n_sub
    sizes = (n_sub, n_grp, own, margins, ncb)
    vm = pltpu.VMEM
    sem = pltpu.SemaphoreType.DMA
    result = pl.pallas_call(
        functools.partial(kernel, sizes),
        out_shape=jax.ShapeDtypeStruct((rows * own, BLK), F32),
        in_specs=[
            pl.BlockSpec(memory_space=pltpu.SMEM),
            pl.BlockSpec(memory_space=pltpu.SMEM),
            pl.BlockSpec(memory_space=pl.ANY),
            pl.BlockSpec(memory_space=pl.ANY),
            pl.BlockSpec(memory_space=pl.ANY),
        ],
        out_specs=pl.BlockSpec(memory_space=pltpu.VMEM),
        scratch_shapes=[
            vm((own * rhs, BLK), F32),
            vm((inner, own_width + margins * BLK), BF16),
            vm(coarse_factor.shape, BF16),
            vm((rows * own, BLK), F32),
            vm((n_sub, rows * margins, BLK), F32),
            vm((n_sub, rows * margins, BLK), F32),
            vm((n_sub, per, (rows + 1) * BLK), F32),
            vm((n_sub, per, (rows + 1) * BLK), F32),
            vm((ncb, rows, BLK), F32),
            vm((n_grp * rows * margins, BLK), F32),
            vm((rhs * inner // BLK, BLK), F32),
            vm((n_grp * rows * margins, BLK), F32),
            vm((n_grp * rows * margins, BLK), F32),
            vm((n_grp * rows * own, BLK), F32),
            vm((n_grp * rows * own, BLK), F32),
            vm((n_sub, rows * margins, BLK), F32),
            vm((ncb, rows, BLK), F32),
            vm((n_sub, per, rows, BLK), F32),
            vm((ncb, rows, BLK), F32),
            vm((rows * own, BLK), F32),
            sem((3,)),
        ] + [sem] * 18,
        compiler_params=pltpu.CompilerParams(collective_id=0, has_side_effects=True),
    )(margin.T, aggregate, residual, local_factor, coarse_factor)
    return result.reshape(own, rows, BLK).transpose(1, 0, 2).reshape(rows, own_width)


def solution(mesh):
    placed = (P(None, "sub"), P(), P("sub"), P("sub", "grp", None), P("sub", None))
    return jax.shard_map(
        on_device, mesh=mesh, in_specs=placed, out_specs=P("grp", "sub"), check_vma=False
    )
```

```python
import functools

import jax
import jax.numpy as jnp
from jax import lax
from jax.experimental import pallas as pl
from jax.experimental.pallas import tpu as pltpu
from jax.sharding import PartitionSpec as P

BLK = 128
F32 = jnp.float32
BF16 = jnp.bfloat16
MESH = pl.DeviceIdType.MESH
NT = (((1,), (1,)), ((), ()))
TN = (((0,), (0,)), ((), ()))


def split(values):
    high = values.astype(BF16)
    return high, (values - high.astype(F32)).astype(BF16)


def split_dot(onehot, values):
    high, low = split(values)
    return jnp.dot(onehot, high, preferred_element_type=F32) + jnp.dot(
        onehot, low, preferred_element_type=F32
    )


def wait_all(ref, sem):
    pltpu.make_async_copy(ref, ref, sem).wait()


def kernel(
    sizes,
    margin, aggregate, residual, local_factor, coarse_factor,
    out,
    margin_v, agg_v, agg_s, res_v, w_v, v_v, mine, pick_out, pick_in, c_out, c_in, c_full, halo, inner_v,
    part_h, recv_h, part_o, recv_o, back, e_part, e_recv, e_full, acc,
    fence, load_sem, pick_send, pick_recv, cs_send, cs_recv, ca_send, ca_recv, halo_send, halo_recv,
    h_send, h_recv, o_send, o_recv, back_send, back_recv, es_send, es_recv, ea_send, ea_recv,
):
    n_sub, n_grp, own, margins, ncb = sizes
    rows = 2
    per = ncb // n_sub
    me = lax.axis_index("sub")
    grp = lax.axis_index("grp")

    barrier = pltpu.get_barrier_semaphore()

    def plane(d):
        return (grp, lax.rem(me + d, n_sub))

    def column(d):
        return (lax.rem(grp + d, n_grp), me)

    for d in range(1, n_sub):
        pl.semaphore_signal(barrier, inc=1, device_id=plane(d), device_id_type=MESH)
    for d in range(1, n_grp):
        pl.semaphore_signal(barrier, inc=1, device_id=column(d), device_id_type=MESH)

    load_margin = pltpu.make_async_copy(margin, margin_v, load_sem.at[3])
    load_agg = pltpu.make_async_copy(aggregate, agg_v, load_sem.at[4])
    load_ids = pltpu.make_async_copy(aggregate, agg_s, load_sem.at[5])
    load_margin.start()
    load_agg.start()
    load_ids.start()
    for b in range(own):
        pltpu.make_async_copy(
            residual.at[:, pl.ds(b * BLK, BLK)],
            res_v.at[pl.ds(b * rows * n_grp, rows * n_grp)],
            load_sem.at[0],
        ).start()
    load_w = pltpu.make_async_copy(local_factor.at[0], w_v, load_sem.at[1])
    load_v = pltpu.make_async_copy(coarse_factor, v_v, load_sem.at[2])
    load_w.start()
    load_v.start()

    def to_plane(src, dst, send, recv):
        for d in range(1, n_sub):
            target = plane(d)
            pltpu.make_async_remote_copy(
                src_ref=src(target[1]), dst_ref=dst, send_sem=send, recv_sem=recv,
                device_id=target, device_id_type=MESH,
            ).start()

    def to_column(src, dst, send, recv):
        for d in range(1, n_grp):
            target = column(d)
            pltpu.make_async_remote_copy(
                src_ref=src(target[0]), dst_ref=dst, send_sem=send, recv_sem=recv,
                device_id=target, device_id_type=MESH,
            ).start()

    def fenced():
        pl.semaphore_signal(fence, 1)
        pl.semaphore_wait(fence, 1)

    slots = n_sub * margins
    each = BLK // n_sub
    lane = lax.broadcasted_iota(jnp.int32, (1, BLK), 1)
    own_ids = lax.broadcasted_iota(jnp.int32, (own, BLK), 0) + me * own
    load_margin.wait()
    spread = jnp.concatenate([margin_v[...]] * each, axis=1)
    tables = []
    for first in range(0, margins, each):
        row = jnp.full((1, BLK), -1, jnp.int32)
        for i in range(min(each, margins - first)):
            here = jnp.logical_and(lane >= i * n_sub, lane < (i + 1) * n_sub)
            row = jnp.where(here, spread[first + i : first + i + 1, :], row)
        tables.append((jnp.broadcast_to(row, (own, BLK)) == own_ids).astype(F32))
    owner_hot = jnp.concatenate(tables, axis=1)[:, :slots]
    load_agg.wait()
    coarse_hot = (
        jnp.broadcast_to(agg_v[...], (ncb, own)) == lax.broadcasted_iota(jnp.int32, (ncb, own), 0)
    ).astype(F32)

    wait_all(res_v, load_sem.at[0])
    for b in range(own):
        for r in range(rows):
            mine[r * own + b : r * own + b + 1, :] = res_v[
                pl.ds(b * rows * n_grp + grp * rows + r, 1), :
            ]
    blocks = jnp.concatenate([mine[r * own : (r + 1) * own, :] for r in range(rows)], axis=1)
    high, low = split(blocks)
    picked = lax.dot_general(owner_hot.astype(BF16), high, TN, preferred_element_type=F32)
    hr = rows * margins
    for r in range(rows):
        for k in range(margins):
            for t in range(0, n_sub, 8):
                at = k * n_sub + t
                pick_out[pl.ds(t * hr + r * margins + k, 8, stride=hr), :] = picked[
                    at : at + 8, r * BLK : (r + 1) * BLK
                ]
    hot = coarse_hot.astype(BF16)
    sums = jnp.dot(hot, high, preferred_element_type=F32) + jnp.dot(
        hot, low, preferred_element_type=F32
    )
    count = jnp.broadcast_to(jnp.sum(coarse_hot, axis=1, keepdims=True), (ncb, BLK))
    sums = jnp.concatenate([sums, count], axis=1)
    for t in range(n_sub):
        c_out[t] = sums[t * per : (t + 1) * per, :]

    pl.semaphore_wait(barrier, n_sub - 1 + n_grp - 1)
    to_plane(lambda t: pick_out.at[pl.ds(t * hr, hr)], pick_in.at[me], pick_send, pick_recv)
    to_plane(lambda t: c_out.at[t], c_in.at[me], cs_send, cs_recv)

    load_w.wait()
    width = own * BLK
    deep = rows * n_grp
    inner = lax.dot_general(
        jnp.concatenate(
            [res_v[b * deep : (b + 1) * deep, :].astype(BF16) for b in range(own)], axis=1
        ),
        w_v[:, :width], NT, preferred_element_type=F32,
    )
    inner_tiles = inner.shape[1] // BLK
    for i in range(inner_tiles):
        inner_v[i * deep : (i + 1) * deep, :] = inner[:, i * BLK : (i + 1) * BLK]

    wait_all(pick_in.at[pl.ds(0, n_sub - 1)], pick_recv)
    pick_in[me] = jnp.zeros((hr, BLK), F32)
    halo[pl.ds(grp * hr, hr)] = jnp.sum(pick_in[...], axis=0)
    mine_halo = halo.at[pl.ds(grp * hr, hr)]
    to_column(lambda t: mine_halo, mine_halo, halo_send, halo_recv)

    wait_all(c_in.at[pl.ds(0, n_sub - 1)], cs_recv)
    c_in[me] = c_out[me]
    sums = jnp.sum(c_in[...], axis=0)
    coarse = sums[:, : rows * BLK] / jnp.maximum(
        jnp.concatenate([sums[:, rows * BLK :]] * rows, axis=1), 1.0
    )
    for i in range(per):
        for r in range(rows):
            c_full[me * per + i, r : r + 1, :] = coarse[i : i + 1, r * BLK : (r + 1) * BLK]
    mine_c = c_full.at[pl.ds(me * per, per)]
    to_plane(lambda t: mine_c, mine_c, ca_send, ca_recv)

    wait_all(halo.at[pl.ds(0, (n_grp - 1) * hr)], halo_recv)
    halo_rhs = jnp.concatenate(
        [
            jnp.concatenate(
                [
                    halo[pl.ds(r * margins + k, n_grp, stride=hr), :]
                    for k in range(margins)
                ],
                axis=1,
            )
            for r in range(rows)
        ],
        axis=0,
    ).astype(BF16)
    inner = jnp.concatenate(
        [
            jnp.concatenate(
                [
                    inner_v[pl.ds(i * deep + r, n_grp, stride=rows), :]
                    for i in range(inner_tiles)
                ],
                axis=1,
            )
            for r in range(rows)
        ],
        axis=0,
    )
    inner = inner + lax.dot_general(halo_rhs, w_v[:, width:], NT, preferred_element_type=F32)
    inner = inner.astype(BF16)
    fenced()

    def scatter_rows(sol, dst, blocks_each):
        for r in range(rows):
            for k in range(blocks_each):
                dst[pl.ds(r * blocks_each + k, n_grp, stride=rows * blocks_each), :] = sol[
                    r * n_grp : (r + 1) * n_grp, k * BLK : (k + 1) * BLK
                ]

    scatter_rows(jnp.dot(inner, w_v[:, width:], preferred_element_type=F32), part_h, margins)
    to_column(
        lambda t: part_h.at[pl.ds(t * hr, hr)], recv_h.at[pl.ds(grp * hr, hr)], h_send, h_recv
    )

    wait_all(c_full.at[pl.ds(0, ncb - per)], ca_recv)
    load_v.wait()
    c_rows = jnp.concatenate([c_full[j] for j in range(ncb)], axis=1).astype(BF16)
    inner_c = lax.dot_general(c_rows, v_v[...], NT, preferred_element_type=F32).astype(BF16)
    fenced()
    e_mine = jnp.dot(inner_c, v_v[...], preferred_element_type=F32)
    for j in range(ncb):
        e_part[j] = e_mine[:, j * BLK : (j + 1) * BLK]
    to_plane(lambda t: e_part.at[pl.ds(t * per, per)], e_recv.at[me], es_send, es_recv)

    scatter_rows(jnp.dot(inner, w_v[:, :width], preferred_element_type=F32), part_o, own)
    orr = rows * own
    to_column(
        lambda t: part_o.at[pl.ds(t * orr, orr)], recv_o.at[pl.ds(grp * orr, orr)], o_send, o_recv
    )

    wait_all(recv_h.at[pl.ds(0, (n_grp - 1) * hr)], h_recv)
    recv_h[pl.ds(grp * hr, hr)] = part_h[pl.ds(grp * hr, hr)]
    mine_back = back.at[pl.ds(me * hr, hr)]
    back[pl.ds(me * hr, hr)] = jnp.sum(recv_h[...].reshape(n_grp, hr, BLK), axis=0)
    to_plane(lambda t: mine_back, mine_back, back_send, back_recv)

    wait_all(e_recv.at[pl.ds(0, n_sub - 1)], es_recv)
    e_recv[me] = e_part[pl.ds(me * per, per)]
    e_full[pl.ds(me * per, per)] = jnp.sum(e_recv[...], axis=0)
    mine_e = e_full.at[pl.ds(me * per, per)]
    to_plane(lambda t: mine_e, mine_e, ea_send, ea_recv)

    wait_all(recv_o.at[pl.ds(0, (n_grp - 1) * orr)], o_recv)
    recv_o[pl.ds(grp * orr, orr)] = part_o[pl.ds(grp * orr, orr)]
    total = jnp.sum(recv_o[...].reshape(n_grp, orr, BLK), axis=0)
    wait_all(e_full.at[pl.ds(0, ncb - per)], ea_recv)
    load_ids.wait()
    for b in range(own):
        acc[b * rows : (b + 1) * rows, :] = e_full[agg_s[0, b]]
    for r in range(rows):
        acc[pl.ds(r, own, stride=rows), :] = (
            acc[pl.ds(r, own, stride=rows), :] + total[r * own : (r + 1) * own, :]
        )

    wait_all(back.at[pl.ds(0, (n_sub - 1) * hr)], back_recv)
    values = jnp.concatenate(
        [
            jnp.concatenate(
                [
                    back[pl.ds(s * hr + r * margins + k, 8, stride=hr), :]
                    for k in range(margins)
                    for s in range(0, n_sub, 8)
                ],
                axis=0,
            )
            for r in range(rows)
        ],
        axis=1,
    )
    returned = split_dot(owner_hot.astype(BF16), values)
    for r in range(rows):
        out[pl.ds(r, own, stride=rows), :] = (
            acc[pl.ds(r, own, stride=rows), :] + returned[:, r * BLK : (r + 1) * BLK]
        )

    wait_all(pick_in.at[pl.ds(0, n_sub - 1)], pick_send)
    wait_all(c_in.at[pl.ds(0, n_sub - 1)], cs_send)
    wait_all(halo.at[pl.ds(0, (n_grp - 1) * hr)], halo_send)
    wait_all(c_full.at[pl.ds(0, ncb - per)], ca_send)
    wait_all(recv_h.at[pl.ds(0, (n_grp - 1) * hr)], h_send)
    wait_all(recv_o.at[pl.ds(0, (n_grp - 1) * orr)], o_send)
    wait_all(e_recv.at[pl.ds(0, n_sub - 1)], es_send)
    wait_all(e_full.at[pl.ds(0, ncb - per)], ea_send)
    wait_all(back.at[pl.ds(0, (n_sub - 1) * hr)], back_send)


def on_device(residual, margin, aggregate, local_factor, coarse_factor):
    n_sub = lax.axis_size("sub")
    n_grp = lax.axis_size("grp")
    rhs, own_width = residual.shape
    own = own_width // BLK
    margins = margin.shape[1]
    inner = local_factor.shape[1]
    ncb = coarse_factor.shape[1] // BLK
    rows = rhs // n_grp
    per = ncb // n_sub
    sizes = (n_sub, n_grp, own, margins, ncb)
    vm = pltpu.VMEM
    sem = pltpu.SemaphoreType.DMA
    result = pl.pallas_call(
        functools.partial(kernel, sizes),
        out_shape=pltpu.VMEM((rows * own, BLK), F32),
        in_specs=[
            pl.BlockSpec(memory_space=pl.ANY),
            pl.BlockSpec(memory_space=pl.ANY),
            pl.BlockSpec(memory_space=pl.ANY),
            pl.BlockSpec(memory_space=pl.ANY),
            pl.BlockSpec(memory_space=pl.ANY),
        ],
        out_specs=pl.BlockSpec(memory_space=pltpu.VMEM),
        scratch_shapes=[
            vm((margins, n_sub), jnp.int32),
            vm((1, own), jnp.int32),
            pltpu.SMEM((1, own), jnp.int32),
            vm((own * rhs, BLK), F32),
            vm((inner, own_width + margins * BLK), BF16),
            vm(coarse_factor.shape, BF16),
            vm((rows * own, BLK), F32),
            vm((n_sub * rows * margins, BLK), F32),
            vm((n_sub, rows * margins, BLK), F32),
            vm((n_sub, per, (rows + 1) * BLK), F32),
            vm((n_sub, per, (rows + 1) * BLK), F32),
            vm((ncb, rows, BLK), F32),
            vm((n_grp * rows * margins, BLK), F32),
            vm((rhs * inner // BLK, BLK), F32),
            vm((n_grp * rows * margins, BLK), F32),
            vm((n_grp * rows * margins, BLK), F32),
            vm((n_grp * rows * own, BLK), F32),
            vm((n_grp * rows * own, BLK), F32),
            vm((n_sub * rows * margins, BLK), F32),
            vm((ncb, rows, BLK), F32),
            vm((n_sub, per, rows, BLK), F32),
            vm((ncb, rows, BLK), F32),
            vm((rows * own, BLK), F32),
            pltpu.SemaphoreType.REGULAR,
            sem((6,)),
        ] + [sem] * 18,
        compiler_params=pltpu.CompilerParams(collective_id=0, has_side_effects=True),
    )(margin.T, aggregate.reshape(1, own), residual, local_factor, coarse_factor)
    return result.reshape(own, rows, BLK).transpose(1, 0, 2).reshape(rows, own_width)


def solution(mesh):
    placed = (P(None, "sub"), P(), P("sub"), P("sub", "grp", None), P("sub", None))
    return jax.shard_map(
        on_device, mesh=mesh, in_specs=placed, out_specs=P("grp", "sub"), check_vma=False
    )
```

```python
import functools

import jax
import jax.numpy as jnp
from jax import lax
from jax.experimental import pallas as pl
from jax.experimental.pallas import tpu as pltpu
from jax.sharding import PartitionSpec as P

BLK = 128
F32 = jnp.float32
BF16 = jnp.bfloat16
MESH = pl.DeviceIdType.MESH
NT = (((1,), (1,)), ((), ()))
TN = (((0,), (0,)), ((), ()))


def split(values):
    high = values.astype(BF16)
    return high, (values - high.astype(F32)).astype(BF16)


def split_dot(onehot, values):
    high, low = split(values)
    return jnp.dot(onehot, high, preferred_element_type=F32) + jnp.dot(
        onehot, low, preferred_element_type=F32
    )


def wait_all(ref, sem):
    pltpu.make_async_copy(ref, ref, sem).wait()


def kernel(
    sizes,
    margin, aggregate, residual, local_factor, coarse_factor,
    out,
    margin_v, agg_v, agg_s, res_v, w_v, v_v, mine, pick_out, pick_in, c_out, c_in, c_full, halo, inner_v,
    part_h, recv_h, part_o, recv_o, back, e_part, e_recv, e_full, acc,
    fence, load_sem, pick_send, pick_recv, cs_send, cs_recv, ca_send, ca_recv, halo_send, halo_recv,
    h_send, h_recv, o_send, o_recv, back_send, back_recv, es_send, es_recv, ea_send, ea_recv,
):
    n_sub, n_grp, own, margins, ncb = sizes
    rows = 2
    per = ncb // n_sub
    me = lax.axis_index("sub")
    grp = lax.axis_index("grp")

    barrier = pltpu.get_barrier_semaphore()

    ny = 4
    nx = n_sub // (2 * ny)
    x = lax.div(me, 2 * ny)
    y = lax.rem(lax.div(me, 2), ny)
    core = lax.rem(me, 2)

    def far(d, n):
        return min(d, n - d)

    steps = [(dx, dy, dc) for dx in range(nx) for dy in range(ny) for dc in range(2)]
    steps = sorted(steps[1:], key=lambda t: -far(t[0], nx) - far(t[1], ny))
    xs = [lax.rem(x + d, nx) * (2 * ny) for d in range(nx)]
    ys = [lax.rem(y + d, ny) * 2 for d in range(ny)]
    cores = [core, 1 - core]
    plane = [(grp, xs[dx] + ys[dy] + cores[dc]) for dx, dy, dc in steps]
    column = [
        (lax.rem(grp + d, n_grp), me) for d in sorted(range(1, n_grp), key=lambda d: -far(d, n_grp))
    ]
    for target in plane + column:
        pl.semaphore_signal(barrier, inc=1, device_id=target, device_id_type=MESH)

    load_margin = pltpu.make_async_copy(margin, margin_v, load_sem.at[3])
    load_agg = pltpu.make_async_copy(aggregate, agg_v, load_sem.at[4])
    load_ids = pltpu.make_async_copy(aggregate, agg_s, load_sem.at[5])
    load_margin.start()
    load_agg.start()
    load_ids.start()
    for b in range(own):
        pltpu.make_async_copy(
            residual.at[:, pl.ds(b * BLK, BLK)],
            res_v.at[pl.ds(b * rows * n_grp, rows * n_grp)],
            load_sem.at[0],
        ).start()
    load_w = pltpu.make_async_copy(local_factor.at[0], w_v, load_sem.at[1])
    load_v = pltpu.make_async_copy(coarse_factor, v_v, load_sem.at[2])
    load_w.start()
    load_v.start()

    def to_plane(src, dst, send, recv):
        for target in plane:
            pltpu.make_async_remote_copy(
                src_ref=src(target[1]), dst_ref=dst, send_sem=send, recv_sem=recv,
                device_id=target, device_id_type=MESH,
            ).start()

    def to_column(src, dst, send, recv):
        for target in column:
            pltpu.make_async_remote_copy(
                src_ref=src(target[0]), dst_ref=dst, send_sem=send, recv_sem=recv,
                device_id=target, device_id_type=MESH,
            ).start()

    def fenced():
        pl.semaphore_signal(fence, 1)
        pl.semaphore_wait(fence, 1)

    slots = n_sub * margins
    each = BLK // n_sub
    lane = lax.broadcasted_iota(jnp.int32, (1, BLK), 1)
    own_ids = lax.broadcasted_iota(jnp.int32, (own, BLK), 0) + me * own
    load_margin.wait()
    spread = jnp.concatenate([margin_v[...]] * each, axis=1)
    tables = []
    for first in range(0, margins, each):
        row = jnp.full((1, BLK), -1, jnp.int32)
        for i in range(min(each, margins - first)):
            here = jnp.logical_and(lane >= i * n_sub, lane < (i + 1) * n_sub)
            row = jnp.where(here, spread[first + i : first + i + 1, :], row)
        tables.append((jnp.broadcast_to(row, (own, BLK)) == own_ids).astype(F32))
    owner_hot = jnp.concatenate(tables, axis=1)[:, :slots]
    load_agg.wait()
    coarse_hot = (
        jnp.broadcast_to(agg_v[...], (ncb, own)) == lax.broadcasted_iota(jnp.int32, (ncb, own), 0)
    ).astype(F32)

    wait_all(res_v, load_sem.at[0])
    for b in range(own):
        for r in range(rows):
            mine[r * own + b : r * own + b + 1, :] = res_v[
                pl.ds(b * rows * n_grp + grp * rows + r, 1), :
            ]
    blocks = jnp.concatenate([mine[r * own : (r + 1) * own, :] for r in range(rows)], axis=1)
    high, low = split(blocks)
    picked = lax.dot_general(owner_hot.astype(BF16), high, TN, preferred_element_type=F32)
    hr = rows * margins
    for r in range(rows):
        for k in range(margins):
            for t in range(0, n_sub, 8):
                at = k * n_sub + t
                pick_out[pl.ds(t * hr + r * margins + k, 8, stride=hr), :] = picked[
                    at : at + 8, r * BLK : (r + 1) * BLK
                ]
    hot = coarse_hot.astype(BF16)
    sums = jnp.dot(hot, high, preferred_element_type=F32) + jnp.dot(
        hot, low, preferred_element_type=F32
    )
    count = jnp.broadcast_to(jnp.sum(coarse_hot, axis=1, keepdims=True), (ncb, BLK))
    sums = jnp.concatenate([sums, count], axis=1)
    for t in range(n_sub):
        c_out[t] = sums[t * per : (t + 1) * per, :]

    pl.semaphore_wait(barrier, n_sub - 1 + n_grp - 1)
    to_plane(lambda t: pick_out.at[pl.ds(t * hr, hr)], pick_in.at[me], pick_send, pick_recv)
    to_plane(lambda t: c_out.at[t], c_in.at[me], cs_send, cs_recv)

    load_w.wait()
    width = own * BLK
    deep = rows * n_grp
    inner = lax.dot_general(
        jnp.concatenate(
            [res_v[b * deep : (b + 1) * deep, :].astype(BF16) for b in range(own)], axis=1
        ),
        w_v[:, :width], NT, preferred_element_type=F32,
    )
    inner_tiles = inner.shape[1] // BLK
    for i in range(inner_tiles):
        inner_v[i * deep : (i + 1) * deep, :] = inner[:, i * BLK : (i + 1) * BLK]

    wait_all(pick_in.at[pl.ds(0, n_sub - 1)], pick_recv)
    pick_in[me] = jnp.zeros((hr, BLK), F32)
    halo[pl.ds(grp * hr, hr)] = jnp.sum(pick_in[...], axis=0)
    mine_halo = halo.at[pl.ds(grp * hr, hr)]
    to_column(lambda t: mine_halo, mine_halo, halo_send, halo_recv)

    wait_all(c_in.at[pl.ds(0, n_sub - 1)], cs_recv)
    c_in[me] = c_out[me]
    sums = jnp.sum(c_in[...], axis=0)
    coarse = sums[:, : rows * BLK] / jnp.maximum(
        jnp.concatenate([sums[:, rows * BLK :]] * rows, axis=1), 1.0
    )
    for i in range(per):
        for r in range(rows):
            c_full[me * per + i, r : r + 1, :] = coarse[i : i + 1, r * BLK : (r + 1) * BLK]
    mine_c = c_full.at[pl.ds(me * per, per)]
    to_plane(lambda t: mine_c, mine_c, ca_send, ca_recv)

    wait_all(halo.at[pl.ds(0, (n_grp - 1) * hr)], halo_recv)
    halo_rhs = jnp.concatenate(
        [
            jnp.concatenate(
                [
                    halo[pl.ds(r * margins + k, n_grp, stride=hr), :]
                    for k in range(margins)
                ],
                axis=1,
            )
            for r in range(rows)
        ],
        axis=0,
    ).astype(BF16)
    inner = jnp.concatenate(
        [
            jnp.concatenate(
                [
                    inner_v[pl.ds(i * deep + r, n_grp, stride=rows), :]
                    for i in range(inner_tiles)
                ],
                axis=1,
            )
            for r in range(rows)
        ],
        axis=0,
    )
    inner = inner + lax.dot_general(halo_rhs, w_v[:, width:], NT, preferred_element_type=F32)
    inner = inner.astype(BF16)
    fenced()

    def scatter_rows(sol, dst, blocks_each):
        for r in range(rows):
            for k in range(blocks_each):
                dst[pl.ds(r * blocks_each + k, n_grp, stride=rows * blocks_each), :] = sol[
                    r * n_grp : (r + 1) * n_grp, k * BLK : (k + 1) * BLK
                ]

    scatter_rows(jnp.dot(inner, w_v[:, width:], preferred_element_type=F32), part_h, margins)
    to_column(
        lambda t: part_h.at[pl.ds(t * hr, hr)], recv_h.at[pl.ds(grp * hr, hr)], h_send, h_recv
    )

    wait_all(c_full.at[pl.ds(0, ncb - per)], ca_recv)
    load_v.wait()
    c_rows = jnp.concatenate([c_full[j] for j in range(ncb)], axis=1).astype(BF16)
    panel = v_v.shape[0]
    inner_c = jnp.concatenate(
        [
            lax.dot_general(
                c_rows, v_v[first : first + panel // 2, :], NT, preferred_element_type=F32
            )
            for first in (0, panel // 2)
        ],
        axis=1,
    ).astype(BF16)
    fenced()
    e_mine = jnp.dot(inner_c, v_v[...], preferred_element_type=F32)
    for j in range(ncb):
        e_part[j] = e_mine[:, j * BLK : (j + 1) * BLK]
    to_plane(lambda t: e_part.at[pl.ds(t * per, per)], e_recv.at[me], es_send, es_recv)

    scatter_rows(jnp.dot(inner, w_v[:, :width], preferred_element_type=F32), part_o, own)
    orr = rows * own
    to_column(
        lambda t: part_o.at[pl.ds(t * orr, orr)], recv_o.at[pl.ds(grp * orr, orr)], o_send, o_recv
    )

    wait_all(recv_h.at[pl.ds(0, (n_grp - 1) * hr)], h_recv)
    recv_h[pl.ds(grp * hr, hr)] = part_h[pl.ds(grp * hr, hr)]
    mine_back = back.at[pl.ds(me * hr, hr)]
    back[pl.ds(me * hr, hr)] = jnp.sum(recv_h[...].reshape(n_grp, hr, BLK), axis=0)
    to_plane(lambda t: mine_back, mine_back, back_send, back_recv)

    wait_all(e_recv.at[pl.ds(0, n_sub - 1)], es_recv)
    e_recv[me] = e_part[pl.ds(me * per, per)]
    e_full[pl.ds(me * per, per)] = jnp.sum(e_recv[...], axis=0)
    mine_e = e_full.at[pl.ds(me * per, per)]
    to_plane(lambda t: mine_e, mine_e, ea_send, ea_recv)

    wait_all(recv_o.at[pl.ds(0, (n_grp - 1) * orr)], o_recv)
    recv_o[pl.ds(grp * orr, orr)] = part_o[pl.ds(grp * orr, orr)]
    total = jnp.sum(recv_o[...].reshape(n_grp, orr, BLK), axis=0)
    wait_all(e_full.at[pl.ds(0, ncb - per)], ea_recv)
    load_ids.wait()
    for b in range(own):
        acc[b * rows : (b + 1) * rows, :] = e_full[agg_s[0, b]]
    for r in range(rows):
        acc[pl.ds(r, own, stride=rows), :] = (
            acc[pl.ds(r, own, stride=rows), :] + total[r * own : (r + 1) * own, :]
        )

    wait_all(back.at[pl.ds(0, (n_sub - 1) * hr)], back_recv)
    values = jnp.concatenate(
        [
            jnp.concatenate(
                [
                    back[pl.ds(s * hr + r * margins + k, 8, stride=hr), :]
                    for k in range(margins)
                    for s in range(0, n_sub, 8)
                ],
                axis=0,
            )
            for r in range(rows)
        ],
        axis=1,
    )
    returned = split_dot(owner_hot.astype(BF16), values)
    for r in range(rows):
        out[pl.ds(r, own, stride=rows), :] = (
            acc[pl.ds(r, own, stride=rows), :] + returned[:, r * BLK : (r + 1) * BLK]
        )

    wait_all(pick_in.at[pl.ds(0, n_sub - 1)], pick_send)
    wait_all(c_in.at[pl.ds(0, n_sub - 1)], cs_send)
    wait_all(halo.at[pl.ds(0, (n_grp - 1) * hr)], halo_send)
    wait_all(c_full.at[pl.ds(0, ncb - per)], ca_send)
    wait_all(recv_h.at[pl.ds(0, (n_grp - 1) * hr)], h_send)
    wait_all(recv_o.at[pl.ds(0, (n_grp - 1) * orr)], o_send)
    wait_all(e_recv.at[pl.ds(0, n_sub - 1)], es_send)
    wait_all(e_full.at[pl.ds(0, ncb - per)], ea_send)
    wait_all(back.at[pl.ds(0, (n_sub - 1) * hr)], back_send)


def on_device(residual, margin, aggregate, local_factor, coarse_factor):
    n_sub = lax.axis_size("sub")
    n_grp = lax.axis_size("grp")
    rhs, own_width = residual.shape
    own = own_width // BLK
    margins = margin.shape[1]
    inner = local_factor.shape[1]
    ncb = coarse_factor.shape[1] // BLK
    rows = rhs // n_grp
    per = ncb // n_sub
    sizes = (n_sub, n_grp, own, margins, ncb)
    vm = pltpu.VMEM
    sem = pltpu.SemaphoreType.DMA
    result = pl.pallas_call(
        functools.partial(kernel, sizes),
        out_shape=pltpu.VMEM((rows * own, BLK), F32),
        in_specs=[
            pl.BlockSpec(memory_space=pl.ANY),
            pl.BlockSpec(memory_space=pl.ANY),
            pl.BlockSpec(memory_space=pl.ANY),
            pl.BlockSpec(memory_space=pl.ANY),
            pl.BlockSpec(memory_space=pl.ANY),
        ],
        out_specs=pl.BlockSpec(memory_space=pltpu.VMEM),
        scratch_shapes=[
            vm((margins, n_sub), jnp.int32),
            vm((1, own), jnp.int32),
            pltpu.SMEM((1, own), jnp.int32),
            vm((own * rhs, BLK), F32),
            vm((inner, own_width + margins * BLK), BF16),
            vm(coarse_factor.shape, BF16),
            vm((rows * own, BLK), F32),
            vm((n_sub * rows * margins, BLK), F32),
            vm((n_sub, rows * margins, BLK), F32),
            vm((n_sub, per, (rows + 1) * BLK), F32),
            vm((n_sub, per, (rows + 1) * BLK), F32),
            vm((ncb, rows, BLK), F32),
            vm((n_grp * rows * margins, BLK), F32),
            vm((rhs * inner // BLK, BLK), F32),
            vm((n_grp * rows * margins, BLK), F32),
            vm((n_grp * rows * margins, BLK), F32),
            vm((n_grp * rows * own, BLK), F32),
            vm((n_grp * rows * own, BLK), F32),
            vm((n_sub * rows * margins, BLK), F32),
            vm((ncb, rows, BLK), F32),
            vm((n_sub, per, rows, BLK), F32),
            vm((ncb, rows, BLK), F32),
            vm((rows * own, BLK), F32),
            pltpu.SemaphoreType.REGULAR,
            sem((6,)),
        ] + [sem] * 18,
        compiler_params=pltpu.CompilerParams(collective_id=0, has_side_effects=True),
    )(margin.T, aggregate.reshape(1, own), residual, local_factor, coarse_factor)
    return result.reshape(own, rows, BLK).transpose(1, 0, 2).reshape(rows, own_width)


def solution(mesh):
    placed = (P(None, "sub"), P(), P("sub"), P("sub", "grp", None), P("sub", None))
    return jax.shard_map(
        on_device, mesh=mesh, in_specs=placed, out_specs=P("grp", "sub"), check_vma=False
    )
```

```python
import functools

import jax
import jax.numpy as jnp
from jax import lax
from jax.experimental import pallas as pl
from jax.experimental.pallas import tpu as pltpu
from jax.sharding import PartitionSpec as P

BLK = 128
F32 = jnp.float32
BF16 = jnp.bfloat16
MESH = pl.DeviceIdType.MESH
NT = (((1,), (1,)), ((), ()))
TN = (((0,), (0,)), ((), ()))


def split(values):
    high = values.astype(BF16)
    return high, (values - high.astype(F32)).astype(BF16)


def split_dot(onehot, values):
    high, low = split(values)
    return jnp.dot(onehot, high, preferred_element_type=F32) + jnp.dot(
        onehot, low, preferred_element_type=F32
    )


def wait_all(ref, sem):
    pltpu.make_async_copy(ref, ref, sem).wait()


def kernel(
    sizes,
    margin, aggregate, residual, local_factor, coarse_factor,
    out,
    margin_v, agg_v, agg_s, res_v, w_v, v_v, vt_v, mine, pick_out, pick_in, c_out, c_in, c_full, halo, inner_v,
    part_h, recv_h, part_o, recv_o, back, e_part, e_recv, e_full, acc,
    fence, load_sem, pick_send, pick_recv, cs_send, cs_recv, ca_send, ca_recv, halo_send, halo_recv,
    h_send, h_recv, o_send, o_recv, back_send, back_recv, es_send, es_recv, ea_send, ea_recv,
):
    n_sub, n_grp, own, margins, ncb = sizes
    rows = 2
    per = ncb // n_sub
    me = lax.axis_index("sub")
    grp = lax.axis_index("grp")

    barrier = pltpu.get_barrier_semaphore()

    ny = 4
    nx = n_sub // (2 * ny)
    x = lax.div(me, 2 * ny)
    y = lax.rem(lax.div(me, 2), ny)
    core = lax.rem(me, 2)

    def far(d, n):
        return min(d, n - d)

    steps = [(dx, dy, dc) for dx in range(nx) for dy in range(ny) for dc in range(2)]
    steps = sorted(steps[1:], key=lambda t: -far(t[0], nx) - far(t[1], ny))
    xs = [lax.rem(x + d, nx) * (2 * ny) for d in range(nx)]
    ys = [lax.rem(y + d, ny) * 2 for d in range(ny)]
    cores = [core, 1 - core]
    plane = [(grp, xs[dx] + ys[dy] + cores[dc]) for dx, dy, dc in steps]
    column = [
        (lax.rem(grp + d, n_grp), me) for d in sorted(range(1, n_grp), key=lambda d: -far(d, n_grp))
    ]
    for target in plane + column:
        pl.semaphore_signal(barrier, inc=1, device_id=target, device_id_type=MESH)

    load_margin = pltpu.make_async_copy(margin, margin_v, load_sem.at[3])
    load_agg = pltpu.make_async_copy(aggregate, agg_v, load_sem.at[4])
    load_ids = pltpu.make_async_copy(aggregate, agg_s, load_sem.at[5])
    load_margin.start()
    load_agg.start()
    load_ids.start()
    for b in range(own):
        pltpu.make_async_copy(
            residual.at[:, pl.ds(b * BLK, BLK)],
            res_v.at[pl.ds(b * rows * n_grp, rows * n_grp)],
            load_sem.at[0],
        ).start()
    load_w = pltpu.make_async_copy(local_factor.at[0], w_v, load_sem.at[1])
    load_v = pltpu.make_async_copy(coarse_factor, v_v, load_sem.at[2])
    load_w.start()
    load_v.start()

    def to_plane(src, dst, send, recv):
        for target in plane:
            pltpu.make_async_remote_copy(
                src_ref=src(target[1]), dst_ref=dst, send_sem=send, recv_sem=recv,
                device_id=target, device_id_type=MESH,
            ).start()

    def to_column(src, dst, send, recv):
        for target in column:
            pltpu.make_async_remote_copy(
                src_ref=src(target[0]), dst_ref=dst, send_sem=send, recv_sem=recv,
                device_id=target, device_id_type=MESH,
            ).start()

    def fenced():
        pl.semaphore_signal(fence, 1)
        pl.semaphore_wait(fence, 1)

    slots = n_sub * margins
    each = BLK // n_sub
    lane = lax.broadcasted_iota(jnp.int32, (1, BLK), 1)
    own_ids = lax.broadcasted_iota(jnp.int32, (own, BLK), 0) + me * own
    load_margin.wait()
    spread = jnp.concatenate([margin_v[...]] * each, axis=1)
    tables = []
    for first in range(0, margins, each):
        row = jnp.full((1, BLK), -1, jnp.int32)
        for i in range(min(each, margins - first)):
            here = jnp.logical_and(lane >= i * n_sub, lane < (i + 1) * n_sub)
            row = jnp.where(here, spread[first + i : first + i + 1, :], row)
        tables.append((jnp.broadcast_to(row, (own, BLK)) == own_ids).astype(F32))
    owner_hot = jnp.concatenate(tables, axis=1)[:, :slots]
    load_agg.wait()
    coarse_hot = (
        jnp.broadcast_to(agg_v[...], (ncb, own)) == lax.broadcasted_iota(jnp.int32, (ncb, own), 0)
    ).astype(F32)

    wait_all(res_v, load_sem.at[0])
    for b in range(own):
        for r in range(rows):
            mine[r * own + b : r * own + b + 1, :] = res_v[
                pl.ds(b * rows * n_grp + grp * rows + r, 1), :
            ]
    blocks = jnp.concatenate([mine[r * own : (r + 1) * own, :] for r in range(rows)], axis=1)
    high, low = split(blocks)
    picked = lax.dot_general(owner_hot.astype(BF16), high, TN, preferred_element_type=F32)
    hr = rows * margins
    for r in range(rows):
        for k in range(margins):
            for t in range(0, n_sub, 8):
                at = k * n_sub + t
                pick_out[pl.ds(t * hr + r * margins + k, 8, stride=hr), :] = picked[
                    at : at + 8, r * BLK : (r + 1) * BLK
                ]
    hot = coarse_hot.astype(BF16)
    sums = jnp.dot(hot, high, preferred_element_type=F32) + jnp.dot(
        hot, low, preferred_element_type=F32
    )
    count = jnp.broadcast_to(jnp.sum(coarse_hot, axis=1, keepdims=True), (ncb, BLK))
    sums = jnp.concatenate([sums, count], axis=1)
    for t in range(n_sub):
        c_out[t] = sums[t * per : (t + 1) * per, :]

    pl.semaphore_wait(barrier, n_sub - 1 + n_grp - 1)
    to_plane(lambda t: pick_out.at[pl.ds(t * hr, hr)], pick_in.at[me], pick_send, pick_recv)
    to_plane(lambda t: c_out.at[t], c_in.at[me], cs_send, cs_recv)

    load_w.wait()
    width = own * BLK
    deep = rows * n_grp
    inner = lax.dot_general(
        jnp.concatenate(
            [res_v[b * deep : (b + 1) * deep, :].astype(BF16) for b in range(own)], axis=1
        ),
        w_v[:, :width], NT, preferred_element_type=F32,
    )
    inner_tiles = inner.shape[1] // BLK
    for i in range(inner_tiles):
        inner_v[i * deep : (i + 1) * deep, :] = inner[:, i * BLK : (i + 1) * BLK]

    load_v.wait()
    tile = 2 * BLK
    panel_tiles = v_v.shape[1] // tile

    def transpose_tiles(begin, end):
        def one(n, carry):
            at = pl.ds(pl.multiple_of(n * tile, tile), tile)
            vt_v[at, :] = v_v[:, at].T
            return carry

        lax.fori_loop(begin, end, one, 0)

    transpose_tiles(0, panel_tiles // 2)

    wait_all(pick_in.at[pl.ds(0, n_sub - 1)], pick_recv)
    pick_in[me] = jnp.zeros((hr, BLK), F32)
    halo[pl.ds(grp * hr, hr)] = jnp.sum(pick_in[...], axis=0)
    mine_halo = halo.at[pl.ds(grp * hr, hr)]
    to_column(lambda t: mine_halo, mine_halo, halo_send, halo_recv)

    wait_all(c_in.at[pl.ds(0, n_sub - 1)], cs_recv)
    c_in[me] = c_out[me]
    sums = jnp.sum(c_in[...], axis=0)
    coarse = sums[:, : rows * BLK] / jnp.maximum(
        jnp.concatenate([sums[:, rows * BLK :]] * rows, axis=1), 1.0
    )
    for i in range(per):
        for r in range(rows):
            c_full[me * per + i, r : r + 1, :] = coarse[i : i + 1, r * BLK : (r + 1) * BLK]
    mine_c = c_full.at[pl.ds(me * per, per)]
    to_plane(lambda t: mine_c, mine_c, ca_send, ca_recv)
    transpose_tiles(panel_tiles // 2, panel_tiles)

    wait_all(halo.at[pl.ds(0, (n_grp - 1) * hr)], halo_recv)
    halo_rhs = jnp.concatenate(
        [
            jnp.concatenate(
                [
                    halo[pl.ds(r * margins + k, n_grp, stride=hr), :]
                    for k in range(margins)
                ],
                axis=1,
            )
            for r in range(rows)
        ],
        axis=0,
    ).astype(BF16)
    inner = jnp.concatenate(
        [
            jnp.concatenate(
                [
                    inner_v[pl.ds(i * deep + r, n_grp, stride=rows), :]
                    for i in range(inner_tiles)
                ],
                axis=1,
            )
            for r in range(rows)
        ],
        axis=0,
    )
    inner = inner + lax.dot_general(halo_rhs, w_v[:, width:], NT, preferred_element_type=F32)
    inner = inner.astype(BF16)
    fenced()

    def scatter_rows(sol, dst, blocks_each):
        for r in range(rows):
            for k in range(blocks_each):
                dst[pl.ds(r * blocks_each + k, n_grp, stride=rows * blocks_each), :] = sol[
                    r * n_grp : (r + 1) * n_grp, k * BLK : (k + 1) * BLK
                ]

    scatter_rows(jnp.dot(inner, w_v[:, width:], preferred_element_type=F32), part_h, margins)
    to_column(
        lambda t: part_h.at[pl.ds(t * hr, hr)], recv_h.at[pl.ds(grp * hr, hr)], h_send, h_recv
    )

    wait_all(c_full.at[pl.ds(0, ncb - per)], ca_recv)
    c_rows = jnp.concatenate([c_full[j] for j in range(ncb)], axis=1).astype(BF16)
    half = v_v.shape[0] // 2
    inner_c = jnp.concatenate(
        [
            jnp.dot(c_rows, vt_v[:, at : at + half], preferred_element_type=F32)
            for at in (0, half)
        ],
        axis=1,
    ).astype(BF16)
    e_mine = jnp.dot(inner_c, v_v[...], preferred_element_type=F32)
    for j in range(ncb):
        e_part[j] = e_mine[:, j * BLK : (j + 1) * BLK]
    to_plane(lambda t: e_part.at[pl.ds(t * per, per)], e_recv.at[me], es_send, es_recv)

    scatter_rows(jnp.dot(inner, w_v[:, :width], preferred_element_type=F32), part_o, own)
    orr = rows * own
    to_column(
        lambda t: part_o.at[pl.ds(t * orr, orr)], recv_o.at[pl.ds(grp * orr, orr)], o_send, o_recv
    )

    wait_all(recv_h.at[pl.ds(0, (n_grp - 1) * hr)], h_recv)
    recv_h[pl.ds(grp * hr, hr)] = part_h[pl.ds(grp * hr, hr)]
    mine_back = back.at[pl.ds(me * hr, hr)]
    back[pl.ds(me * hr, hr)] = jnp.sum(recv_h[...].reshape(n_grp, hr, BLK), axis=0)
    to_plane(lambda t: mine_back, mine_back, back_send, back_recv)

    wait_all(e_recv.at[pl.ds(0, n_sub - 1)], es_recv)
    e_recv[me] = e_part[pl.ds(me * per, per)]
    e_full[pl.ds(me * per, per)] = jnp.sum(e_recv[...], axis=0)
    mine_e = e_full.at[pl.ds(me * per, per)]
    to_plane(lambda t: mine_e, mine_e, ea_send, ea_recv)

    wait_all(recv_o.at[pl.ds(0, (n_grp - 1) * orr)], o_recv)
    recv_o[pl.ds(grp * orr, orr)] = part_o[pl.ds(grp * orr, orr)]
    total = jnp.sum(recv_o[...].reshape(n_grp, orr, BLK), axis=0)
    wait_all(back.at[pl.ds(0, (n_sub - 1) * hr)], back_recv)
    values = jnp.concatenate(
        [
            jnp.concatenate(
                [
                    back[pl.ds(s * hr + r * margins + k, 8, stride=hr), :]
                    for k in range(margins)
                    for s in range(0, n_sub, 8)
                ],
                axis=0,
            )
            for r in range(rows)
        ],
        axis=1,
    )
    returned = split_dot(owner_hot.astype(BF16), values)
    for r in range(rows):
        acc[pl.ds(r, own, stride=rows), :] = (
            total[r * own : (r + 1) * own, :] + returned[:, r * BLK : (r + 1) * BLK]
        )
    load_ids.wait()
    wait_all(e_full.at[pl.ds(0, ncb - per)], ea_recv)
    for b in range(own):
        j = agg_s[0, b]
        at = slice(b * rows, (b + 1) * rows)
        out[at, :] = acc[at, :] + e_full[j]

    wait_all(pick_in.at[pl.ds(0, n_sub - 1)], pick_send)
    wait_all(c_in.at[pl.ds(0, n_sub - 1)], cs_send)
    wait_all(halo.at[pl.ds(0, (n_grp - 1) * hr)], halo_send)
    wait_all(c_full.at[pl.ds(0, ncb - per)], ca_send)
    wait_all(recv_h.at[pl.ds(0, (n_grp - 1) * hr)], h_send)
    wait_all(recv_o.at[pl.ds(0, (n_grp - 1) * orr)], o_send)
    wait_all(e_recv.at[pl.ds(0, n_sub - 1)], es_send)
    wait_all(e_full.at[pl.ds(0, ncb - per)], ea_send)
    wait_all(back.at[pl.ds(0, (n_sub - 1) * hr)], back_send)


def on_device(residual, margin, aggregate, local_factor, coarse_factor):
    n_sub = lax.axis_size("sub")
    n_grp = lax.axis_size("grp")
    rhs, own_width = residual.shape
    own = own_width // BLK
    margins = margin.shape[1]
    inner = local_factor.shape[1]
    ncb = coarse_factor.shape[1] // BLK
    rows = rhs // n_grp
    per = ncb // n_sub
    sizes = (n_sub, n_grp, own, margins, ncb)
    vm = pltpu.VMEM
    sem = pltpu.SemaphoreType.DMA
    result = pl.pallas_call(
        functools.partial(kernel, sizes),
        out_shape=pltpu.VMEM((rows * own, BLK), F32),
        in_specs=[
            pl.BlockSpec(memory_space=pl.ANY),
            pl.BlockSpec(memory_space=pl.ANY),
            pl.BlockSpec(memory_space=pl.ANY),
            pl.BlockSpec(memory_space=pl.ANY),
            pl.BlockSpec(memory_space=pl.ANY),
        ],
        out_specs=pl.BlockSpec(memory_space=pltpu.VMEM),
        scratch_shapes=[
            vm((margins, n_sub), jnp.int32),
            vm((1, own), jnp.int32),
            pltpu.SMEM((1, own), jnp.int32),
            vm((own * rhs, BLK), F32),
            vm((inner, own_width + margins * BLK), BF16),
            vm(coarse_factor.shape, BF16),
            vm(coarse_factor.shape[::-1], BF16),
            vm((rows * own, BLK), F32),
            vm((n_sub * rows * margins, BLK), F32),
            vm((n_sub, rows * margins, BLK), F32),
            vm((n_sub, per, (rows + 1) * BLK), F32),
            vm((n_sub, per, (rows + 1) * BLK), F32),
            vm((ncb, rows, BLK), F32),
            vm((n_grp * rows * margins, BLK), F32),
            vm((rhs * inner // BLK, BLK), F32),
            vm((n_grp * rows * margins, BLK), F32),
            vm((n_grp * rows * margins, BLK), F32),
            vm((n_grp * rows * own, BLK), F32),
            vm((n_grp * rows * own, BLK), F32),
            vm((n_sub * rows * margins, BLK), F32),
            vm((ncb, rows, BLK), F32),
            vm((n_sub, per, rows, BLK), F32),
            vm((ncb, rows, BLK), F32),
            vm((rows * own, BLK), F32),
            pltpu.SemaphoreType.REGULAR,
            sem((6,)),
        ] + [sem] * 18,
        compiler_params=pltpu.CompilerParams(collective_id=0, has_side_effects=True),
    )(margin.T, aggregate.reshape(1, own), residual, local_factor, coarse_factor)
    return result.reshape(own, rows, BLK).transpose(1, 0, 2).reshape(rows, own_width)


def solution(mesh):
    placed = (P(None, "sub"), P(), P("sub"), P("sub", "grp", None), P("sub", None))
    return jax.shard_map(
        on_device, mesh=mesh, in_specs=placed, out_specs=P("grp", "sub"), check_vma=False
    )
```

```python
import functools

import jax
import jax.numpy as jnp
from jax import lax
from jax.experimental import pallas as pl
from jax.experimental.pallas import tpu as pltpu
from jax.sharding import PartitionSpec as P

BLK = 128
F32 = jnp.float32
BF16 = jnp.bfloat16
MESH = pl.DeviceIdType.MESH
NT = (((1,), (1,)), ((), ()))
TN = (((0,), (0,)), ((), ()))


def split(values):
    high = values.astype(BF16)
    return high, (values - high.astype(F32)).astype(BF16)


def split_dot(onehot, values):
    high, low = split(values)
    return jnp.dot(onehot, high, preferred_element_type=F32) + jnp.dot(
        onehot, low, preferred_element_type=F32
    )


def wait_all(ref, sem):
    pltpu.make_async_copy(ref, ref, sem).wait()


def kernel(
    sizes,
    margin, aggregate, residual, local_factor, coarse_factor,
    out,
    margin_v, agg_v, agg_s, res_v, w_v, v_v, vt_v, wt_v, mine, pick_out, pick_in, c_out, c_in, c_full, halo, inner_v,
    part_h, recv_h, part_o, recv_o, back, e_part, e_recv, e_full, acc,
    load_sem, pick_send, pick_recv, cs_send, cs_recv, ca_send, ca_recv, halo_send, halo_recv,
    h_send, h_recv, o_send, o_recv, back_send, back_recv, es_send, es_recv, ea_send, ea_recv,
):
    n_sub, n_grp, own, margins, ncb = sizes
    rows = 2
    per = ncb // n_sub
    me = lax.axis_index("sub")
    grp = lax.axis_index("grp")

    barrier = pltpu.get_barrier_semaphore()

    ny = 4
    nx = n_sub // (2 * ny)
    x = lax.div(me, 2 * ny)
    y = lax.rem(lax.div(me, 2), ny)
    core = lax.rem(me, 2)

    def far(d, n):
        return min(d, n - d)

    steps = [(dx, dy, dc) for dx in range(nx) for dy in range(ny) for dc in range(2)]
    steps = sorted(steps[1:], key=lambda t: -far(t[0], nx) - far(t[1], ny))
    xs = [lax.rem(x + d, nx) * (2 * ny) for d in range(nx)]
    ys = [lax.rem(y + d, ny) * 2 for d in range(ny)]
    cores = [core, 1 - core]
    plane = [(grp, xs[dx] + ys[dy] + cores[dc]) for dx, dy, dc in steps]
    column = [
        (lax.rem(grp + d, n_grp), me) for d in sorted(range(1, n_grp), key=lambda d: -far(d, n_grp))
    ]
    far_z = [far(d, n_grp) for d in sorted(range(1, n_grp), key=lambda d: -far(d, n_grp))]
    far_p = [far(dx, nx) + far(dy, ny) for dx, dy, _ in steps]
    ranked = sorted(zip(far_z + far_p, range(len(far_z + far_p))), key=lambda t: -t[0])
    for target in [(column + plane)[i] for _, i in ranked]:
        pl.semaphore_signal(barrier, inc=1, device_id=target, device_id_type=MESH)

    load_margin = pltpu.make_async_copy(margin, margin_v, load_sem.at[3])
    load_agg = pltpu.make_async_copy(aggregate, agg_v, load_sem.at[4])
    load_ids = pltpu.make_async_copy(aggregate, agg_s, load_sem.at[5])
    load_margin.start()
    load_agg.start()
    load_ids.start()
    for b in range(own):
        pltpu.make_async_copy(
            residual.at[:, pl.ds(b * BLK, BLK)],
            res_v.at[pl.ds(b * rows * n_grp, rows * n_grp)],
            load_sem.at[0],
        ).start()
    load_w = pltpu.make_async_copy(local_factor.at[0], w_v, load_sem.at[1])
    load_v = pltpu.make_async_copy(coarse_factor, v_v, load_sem.at[2])
    load_w.start()
    load_v.start()

    def to_plane(src, dst, send, recv):
        for target in plane:
            pltpu.make_async_remote_copy(
                src_ref=src(target[1]), dst_ref=dst, send_sem=send, recv_sem=recv,
                device_id=target, device_id_type=MESH,
            ).start()

    def to_column(src, dst, send, recv):
        for target in column:
            pltpu.make_async_remote_copy(
                src_ref=src(target[0]), dst_ref=dst, send_sem=send, recv_sem=recv,
                device_id=target, device_id_type=MESH,
            ).start()

    slots = n_sub * margins
    each = BLK // n_sub
    lane = lax.broadcasted_iota(jnp.int32, (1, BLK), 1)
    own_ids = lax.broadcasted_iota(jnp.int32, (own, BLK), 0) + me * own
    load_margin.wait()
    spread = jnp.concatenate([margin_v[...]] * each, axis=1)
    tables = []
    for first in range(0, margins, each):
        row = jnp.full((1, BLK), -1, jnp.int32)
        for i in range(min(each, margins - first)):
            here = jnp.logical_and(lane >= i * n_sub, lane < (i + 1) * n_sub)
            row = jnp.where(here, spread[first + i : first + i + 1, :], row)
        tables.append((jnp.broadcast_to(row, (own, BLK)) == own_ids).astype(F32))
    owner_hot = jnp.concatenate(tables, axis=1)[:, :slots]
    load_agg.wait()
    coarse_hot = (
        jnp.broadcast_to(agg_v[...], (ncb, own)) == lax.broadcasted_iota(jnp.int32, (ncb, own), 0)
    ).astype(F32)

    wait_all(res_v, load_sem.at[0])
    for b in range(own):
        for r in range(rows):
            mine[r * own + b : r * own + b + 1, :] = res_v[
                pl.ds(b * rows * n_grp + grp * rows + r, 1), :
            ]
    blocks = jnp.concatenate([mine[r * own : (r + 1) * own, :] for r in range(rows)], axis=1)
    high, low = split(blocks)
    picked = lax.dot_general(owner_hot.astype(BF16), high, TN, preferred_element_type=F32)
    hr = rows * margins
    for r in range(rows):
        for k in range(margins):
            for t in range(0, n_sub, 8):
                at = k * n_sub + t
                pick_out[pl.ds(t * hr + r * margins + k, 8, stride=hr), :] = picked[
                    at : at + 8, r * BLK : (r + 1) * BLK
                ]
    hot = coarse_hot.astype(BF16)
    sums = jnp.dot(hot, high, preferred_element_type=F32) + jnp.dot(
        hot, low, preferred_element_type=F32
    )
    count = jnp.broadcast_to(jnp.sum(coarse_hot, axis=1, keepdims=True), (ncb, BLK))
    sums = jnp.concatenate([sums, count], axis=1)
    for t in range(n_sub):
        c_out[t] = sums[t * per : (t + 1) * per, :]

    pl.semaphore_wait(barrier, n_sub - 1 + n_grp - 1)
    to_plane(lambda t: pick_out.at[pl.ds(t * hr, hr)], pick_in.at[me], pick_send, pick_recv)
    to_plane(lambda t: c_out.at[t], c_in.at[me], cs_send, cs_recv)

    load_w.wait()
    width = own * BLK
    deep = rows * n_grp
    inner = lax.dot_general(
        jnp.concatenate(
            [res_v[b * deep : (b + 1) * deep, :].astype(BF16) for b in range(own)], axis=1
        ),
        w_v[:, :width], NT, preferred_element_type=F32,
    )
    inner_tiles = inner.shape[1] // BLK
    for i in range(inner_tiles):
        inner_v[i * deep : (i + 1) * deep, :] = inner[:, i * BLK : (i + 1) * BLK]

    for k in range(0, margins, 2):
        at = k * BLK
        wt_v[at : at + 2 * BLK, :] = w_v[:, width + at : width + at + 2 * BLK].T

    load_v.wait()
    tile = 2 * BLK
    panel_tiles = v_v.shape[1] // tile

    def transpose_tiles(begin, end):
        def one(n, carry):
            at = pl.ds(pl.multiple_of(n * tile, tile), tile)
            vt_v[at, :] = v_v[:, at].T
            return carry

        lax.fori_loop(begin, end, one, 0)

    transpose_tiles(0, panel_tiles // 2)

    wait_all(pick_in.at[pl.ds(0, n_sub - 1)], pick_recv)
    pick_in[me] = jnp.zeros((hr, BLK), F32)
    halo[pl.ds(grp * hr, hr)] = jnp.sum(pick_in[...], axis=0)
    mine_halo = halo.at[pl.ds(grp * hr, hr)]
    to_column(lambda t: mine_halo, mine_halo, halo_send, halo_recv)

    wait_all(c_in.at[pl.ds(0, n_sub - 1)], cs_recv)
    c_in[me] = c_out[me]
    sums = jnp.sum(c_in[...], axis=0)
    coarse = sums[:, : rows * BLK] / jnp.maximum(
        jnp.concatenate([sums[:, rows * BLK :]] * rows, axis=1), 1.0
    )
    for i in range(per):
        for r in range(rows):
            c_full[me * per + i, r : r + 1, :] = coarse[i : i + 1, r * BLK : (r + 1) * BLK]
    mine_c = c_full.at[pl.ds(me * per, per)]
    to_plane(lambda t: mine_c, mine_c, ca_send, ca_recv)
    transpose_tiles(panel_tiles // 2, panel_tiles)

    wait_all(halo.at[pl.ds(0, (n_grp - 1) * hr)], halo_recv)
    halo_rhs = jnp.concatenate(
        [
            jnp.concatenate(
                [
                    halo[pl.ds(r * margins + k, n_grp, stride=hr), :]
                    for k in range(margins)
                ],
                axis=1,
            )
            for r in range(rows)
        ],
        axis=0,
    ).astype(BF16)
    inner = jnp.concatenate(
        [
            jnp.concatenate(
                [
                    inner_v[pl.ds(i * deep + r, n_grp, stride=rows), :]
                    for i in range(inner_tiles)
                ],
                axis=1,
            )
            for r in range(rows)
        ],
        axis=0,
    )
    inner = inner + jnp.dot(halo_rhs, wt_v[...], preferred_element_type=F32)
    inner = inner.astype(BF16)

    def scatter_rows(sol, dst, blocks_each):
        for r in range(rows):
            for k in range(blocks_each):
                dst[pl.ds(r * blocks_each + k, n_grp, stride=rows * blocks_each), :] = sol[
                    r * n_grp : (r + 1) * n_grp, k * BLK : (k + 1) * BLK
                ]

    scatter_rows(jnp.dot(inner, w_v[:, width:], preferred_element_type=F32), part_h, margins)
    to_column(
        lambda t: part_h.at[pl.ds(t * hr, hr)], recv_h.at[pl.ds(grp * hr, hr)], h_send, h_recv
    )

    wait_all(c_full.at[pl.ds(0, ncb - per)], ca_recv)
    c_rows = jnp.concatenate([c_full[j] for j in range(ncb)], axis=1).astype(BF16)
    half = v_v.shape[0] // 2
    inner_c = jnp.concatenate(
        [
            jnp.dot(c_rows, vt_v[:, at : at + half], preferred_element_type=F32)
            for at in (0, half)
        ],
        axis=1,
    ).astype(BF16)
    e_mine = jnp.dot(inner_c, v_v[...], preferred_element_type=F32)
    for j in range(ncb):
        e_part[j] = e_mine[:, j * BLK : (j + 1) * BLK]
    to_plane(lambda t: e_part.at[pl.ds(t * per, per)], e_recv.at[me], es_send, es_recv)

    scatter_rows(jnp.dot(inner, w_v[:, :width], preferred_element_type=F32), part_o, own)
    orr = rows * own
    to_column(
        lambda t: part_o.at[pl.ds(t * orr, orr)], recv_o.at[pl.ds(grp * orr, orr)], o_send, o_recv
    )

    wait_all(recv_h.at[pl.ds(0, (n_grp - 1) * hr)], h_recv)
    recv_h[pl.ds(grp * hr, hr)] = part_h[pl.ds(grp * hr, hr)]
    mine_back = back.at[pl.ds(me * hr, hr)]
    back[pl.ds(me * hr, hr)] = jnp.sum(recv_h[...].reshape(n_grp, hr, BLK), axis=0)
    to_plane(lambda t: mine_back, mine_back, back_send, back_recv)

    wait_all(e_recv.at[pl.ds(0, n_sub - 1)], es_recv)
    e_recv[me] = e_part[pl.ds(me * per, per)]
    e_full[pl.ds(me * per, per)] = jnp.sum(e_recv[...], axis=0)
    mine_e = e_full.at[pl.ds(me * per, per)]
    to_plane(lambda t: mine_e, mine_e, ea_send, ea_recv)

    wait_all(recv_o.at[pl.ds(0, (n_grp - 1) * orr)], o_recv)
    recv_o[pl.ds(grp * orr, orr)] = part_o[pl.ds(grp * orr, orr)]
    total = jnp.sum(recv_o[...].reshape(n_grp, orr, BLK), axis=0)
    wait_all(back.at[pl.ds(0, (n_sub - 1) * hr)], back_recv)
    values = jnp.concatenate(
        [
            jnp.concatenate(
                [
                    back[pl.ds(s * hr + r * margins + k, 8, stride=hr), :]
                    for k in range(margins)
                    for s in range(0, n_sub, 8)
                ],
                axis=0,
            )
            for r in range(rows)
        ],
        axis=1,
    )
    returned = split_dot(owner_hot.astype(BF16), values)
    for r in range(rows):
        acc[pl.ds(r, own, stride=rows), :] = (
            total[r * own : (r + 1) * own, :] + returned[:, r * BLK : (r + 1) * BLK]
        )
    load_ids.wait()
    wait_all(e_full.at[pl.ds(0, ncb - per)], ea_recv)
    for b in range(own):
        j = agg_s[0, b]
        at = slice(b * rows, (b + 1) * rows)
        out[at, :] = acc[at, :] + e_full[j]

    wait_all(pick_in.at[pl.ds(0, n_sub - 1)], pick_send)
    wait_all(c_in.at[pl.ds(0, n_sub - 1)], cs_send)
    wait_all(halo.at[pl.ds(0, (n_grp - 1) * hr)], halo_send)
    wait_all(c_full.at[pl.ds(0, ncb - per)], ca_send)
    wait_all(recv_h.at[pl.ds(0, (n_grp - 1) * hr)], h_send)
    wait_all(recv_o.at[pl.ds(0, (n_grp - 1) * orr)], o_send)
    wait_all(e_recv.at[pl.ds(0, n_sub - 1)], es_send)
    wait_all(e_full.at[pl.ds(0, ncb - per)], ea_send)
    wait_all(back.at[pl.ds(0, (n_sub - 1) * hr)], back_send)


def on_device(residual, margin, aggregate, local_factor, coarse_factor):
    n_sub = lax.axis_size("sub")
    n_grp = lax.axis_size("grp")
    rhs, own_width = residual.shape
    own = own_width // BLK
    margins = margin.shape[1]
    inner = local_factor.shape[1]
    ncb = coarse_factor.shape[1] // BLK
    rows = rhs // n_grp
    per = ncb // n_sub
    sizes = (n_sub, n_grp, own, margins, ncb)
    vm = pltpu.VMEM
    sem = pltpu.SemaphoreType.DMA
    result = pl.pallas_call(
        functools.partial(kernel, sizes),
        out_shape=pltpu.VMEM((rows * own, BLK), F32),
        in_specs=[
            pl.BlockSpec(memory_space=pl.ANY),
            pl.BlockSpec(memory_space=pl.ANY),
            pl.BlockSpec(memory_space=pl.ANY),
            pl.BlockSpec(memory_space=pl.ANY),
            pl.BlockSpec(memory_space=pl.ANY),
        ],
        out_specs=pl.BlockSpec(memory_space=pltpu.VMEM),
        scratch_shapes=[
            vm((margins, n_sub), jnp.int32),
            vm((1, own), jnp.int32),
            pltpu.SMEM((1, own), jnp.int32),
            vm((own * rhs, BLK), F32),
            vm((inner, own_width + margins * BLK), BF16),
            vm(coarse_factor.shape, BF16),
            vm(coarse_factor.shape[::-1], BF16),
            vm((margins * BLK, inner), BF16),
            vm((rows * own, BLK), F32),
            vm((n_sub * rows * margins, BLK), F32),
            vm((n_sub, rows * margins, BLK), F32),
            vm((n_sub, per, (rows + 1) * BLK), F32),
            vm((n_sub, per, (rows + 1) * BLK), F32),
            vm((ncb, rows, BLK), F32),
            vm((n_grp * rows * margins, BLK), F32),
            vm((rhs * inner // BLK, BLK), F32),
            vm((n_grp * rows * margins, BLK), F32),
            vm((n_grp * rows * margins, BLK), F32),
            vm((n_grp * rows * own, BLK), F32),
            vm((n_grp * rows * own, BLK), F32),
            vm((n_sub * rows * margins, BLK), F32),
            vm((ncb, rows, BLK), F32),
            vm((n_sub, per, rows, BLK), F32),
            vm((ncb, rows, BLK), F32),
            vm((rows * own, BLK), F32),
            sem((6,)),
        ] + [sem] * 18,
        compiler_params=pltpu.CompilerParams(collective_id=0, has_side_effects=True),
    )(margin.T, aggregate.reshape(1, own), residual, local_factor, coarse_factor)
    return result.reshape(own, rows, BLK).transpose(1, 0, 2).reshape(rows, own_width)


def solution(mesh):
    placed = (P(None, "sub"), P(), P("sub"), P("sub", "grp", None), P("sub", None))
    return jax.shard_map(
        on_device, mesh=mesh, in_specs=placed, out_specs=P("grp", "sub"), check_vma=False
    )
```

```python
import functools

import jax
import jax.numpy as jnp
from jax import lax
from jax.experimental import pallas as pl
from jax.experimental.pallas import tpu as pltpu
from jax.sharding import PartitionSpec as P

BLK = 128
F32 = jnp.float32
BF16 = jnp.bfloat16
MESH = pl.DeviceIdType.MESH
NT = (((1,), (1,)), ((), ()))
TN = (((0,), (0,)), ((), ()))


def split(values):
    high = values.astype(BF16)
    return high, (values - high.astype(F32)).astype(BF16)


def split_dot(onehot, values):
    high, low = split(values)
    return jnp.dot(onehot, high, preferred_element_type=F32) + jnp.dot(
        onehot, low, preferred_element_type=F32
    )


def wait_all(ref, sem):
    pltpu.make_async_copy(ref, ref, sem).wait()


def kernel(
    sizes,
    margin, aggregate, residual, local_factor, coarse_factor,
    out,
    margin_v, agg_v, agg_s, res_v, w_v, v_v, vt_v, wt_v, mine, pick_out, pick_in, c_out, c_in, c_full, halo, inner_v,
    part_h, recv_h, part_o, recv_o, back, e_part, e_recv, e_full, acc,
    load_sem, pick_send, pick_recv, cs_send, cs_recv, ca_send, ca_recv, halo_send, halo_recv,
    h_send, h_recv, o_send, o_recv, back_send, back_recv, es_send, es_recv, ea_send, ea_recv,
):
    n_sub, n_grp, own, margins, ncb = sizes
    rows = 2
    per = ncb // n_sub
    me = lax.axis_index("sub")
    grp = lax.axis_index("grp")

    barrier = pltpu.get_barrier_semaphore()

    ny = 4
    nx = n_sub // (2 * ny)
    x = lax.div(me, 2 * ny)
    y = lax.rem(lax.div(me, 2), ny)
    core = lax.rem(me, 2)

    def far(d, n):
        return min(d, n - d)

    steps = [(dx, dy, dc) for dx in range(nx) for dy in range(ny) for dc in range(2)]
    steps = sorted(steps[1:], key=lambda t: -far(t[0], nx) - far(t[1], ny))
    xs = [lax.rem(x + d, nx) * (2 * ny) for d in range(nx)]
    ys = [lax.rem(y + d, ny) * 2 for d in range(ny)]
    cores = [core, 1 - core]
    plane = [(grp, xs[dx] + ys[dy] + cores[dc]) for dx, dy, dc in steps]
    column = [
        (lax.rem(grp + d, n_grp), me) for d in sorted(range(1, n_grp), key=lambda d: -far(d, n_grp))
    ]
    far_z = [far(d, n_grp) for d in sorted(range(1, n_grp), key=lambda d: -far(d, n_grp))]
    far_p = [far(dx, nx) + far(dy, ny) for dx, dy, _ in steps]
    ranked = sorted(zip(far_z + far_p, range(len(far_z + far_p))), key=lambda t: -t[0])
    for target in [(column + plane)[i] for _, i in ranked]:
        pl.semaphore_signal(barrier, inc=1, device_id=target, device_id_type=MESH)

    load_margin = pltpu.make_async_copy(margin, margin_v, load_sem.at[3])
    load_agg = pltpu.make_async_copy(aggregate, agg_v, load_sem.at[4])
    load_ids = pltpu.make_async_copy(aggregate, agg_s, load_sem.at[5])
    load_margin.start()
    load_agg.start()
    load_ids.start()
    for b in range(own):
        pltpu.make_async_copy(
            residual.at[:, pl.ds(b * BLK, BLK)],
            res_v.at[pl.ds(b * rows * n_grp, rows * n_grp)],
            load_sem.at[0],
        ).start()
    load_w = pltpu.make_async_copy(local_factor.at[0], w_v, load_sem.at[1])
    load_v = pltpu.make_async_copy(coarse_factor, v_v, load_sem.at[2])
    load_w.start()
    load_v.start()

    def to_plane(src, dst, send, recv):
        for target in plane:
            pltpu.make_async_remote_copy(
                src_ref=src(target[1]), dst_ref=dst, send_sem=send, recv_sem=recv,
                device_id=target, device_id_type=MESH,
            ).start()

    def to_column(src, dst, send, recv):
        for target in column:
            pltpu.make_async_remote_copy(
                src_ref=src(target[0]), dst_ref=dst, send_sem=send, recv_sem=recv,
                device_id=target, device_id_type=MESH,
            ).start()

    slots = n_sub * margins
    each = BLK // n_sub
    lane = lax.broadcasted_iota(jnp.int32, (1, BLK), 1)
    own_ids = lax.broadcasted_iota(jnp.int32, (own, BLK), 0) + me * own
    load_margin.wait()
    spread = jnp.concatenate([margin_v[...]] * each, axis=1)
    tables = []
    for first in range(0, margins, each):
        row = jnp.full((1, BLK), -1, jnp.int32)
        for i in range(min(each, margins - first)):
            here = jnp.logical_and(lane >= i * n_sub, lane < (i + 1) * n_sub)
            row = jnp.where(here, spread[first + i : first + i + 1, :], row)
        tables.append((jnp.broadcast_to(row, (own, BLK)) == own_ids).astype(F32))
    owner_hot = jnp.concatenate(tables, axis=1)[:, :slots]
    load_agg.wait()
    coarse_hot = (
        jnp.broadcast_to(agg_v[...], (ncb, own)) == lax.broadcasted_iota(jnp.int32, (ncb, own), 0)
    ).astype(F32)

    wait_all(res_v, load_sem.at[0])
    for b in range(own):
        for r in range(rows):
            mine[r * own + b : r * own + b + 1, :] = res_v[
                pl.ds(b * rows * n_grp + grp * rows + r, 1), :
            ]
    blocks = jnp.concatenate([mine[r * own : (r + 1) * own, :] for r in range(rows)], axis=1)
    high, low = split(blocks)
    picked = lax.dot_general(owner_hot.astype(BF16), high, TN, preferred_element_type=F32)
    hr = rows * margins
    for r in range(rows):
        for k in range(margins):
            for t in range(0, n_sub, 8):
                at = k * n_sub + t
                pick_out[pl.ds(t * hr + r * margins + k, 8, stride=hr), :] = picked[
                    at : at + 8, r * BLK : (r + 1) * BLK
                ]
    hot = coarse_hot.astype(BF16)
    sums = jnp.dot(hot, high, preferred_element_type=F32) + jnp.dot(
        hot, low, preferred_element_type=F32
    )
    count = jnp.broadcast_to(jnp.sum(coarse_hot, axis=1, keepdims=True), (ncb, BLK))
    sums = jnp.concatenate([sums, count], axis=1)
    for t in range(n_sub):
        c_out[t] = sums[t * per : (t + 1) * per, :]

    pl.semaphore_wait(barrier, n_sub - 1 + n_grp - 1)
    to_plane(lambda t: pick_out.at[pl.ds(t * hr, hr)], pick_in.at[me], pick_send, pick_recv)
    to_plane(lambda t: c_out.at[t], c_in.at[me], cs_send, cs_recv)

    load_w.wait()
    width = own * BLK
    deep = rows * n_grp
    inner = lax.dot_general(
        jnp.concatenate(
            [res_v[b * deep : (b + 1) * deep, :].astype(BF16) for b in range(own)], axis=1
        ),
        w_v[:, :width], NT, preferred_element_type=F32,
    )
    inner_tiles = inner.shape[1] // BLK
    for i in range(inner_tiles):
        inner_v[i * deep : (i + 1) * deep, :] = inner[:, i * BLK : (i + 1) * BLK]

    for k in range(0, margins, 2):
        at = k * BLK
        wt_v[at : at + 2 * BLK, :] = w_v[:, width + at : width + at + 2 * BLK].T

    load_v.wait()
    tile = 2 * BLK
    panel_tiles = v_v.shape[1] // tile

    def transpose_tiles(begin, end):
        def one(n, carry):
            at = pl.ds(pl.multiple_of(n * tile, tile), tile)
            vt_v[at, :] = v_v[:, at].T
            return carry

        lax.fori_loop(begin, end, one, 0)

    transpose_tiles(0, panel_tiles * 3 // 4)

    wait_all(pick_in.at[pl.ds(0, n_sub - 1)], pick_recv)
    pick_in[me] = jnp.zeros((hr, BLK), F32)
    halo[pl.ds(grp * hr, hr)] = jnp.sum(pick_in[...], axis=0)
    mine_halo = halo.at[pl.ds(grp * hr, hr)]
    to_column(lambda t: mine_halo, mine_halo, halo_send, halo_recv)

    wait_all(c_in.at[pl.ds(0, n_sub - 1)], cs_recv)
    c_in[me] = c_out[me]
    sums = jnp.sum(c_in[...], axis=0)
    coarse = sums[:, : rows * BLK] / jnp.maximum(
        jnp.concatenate([sums[:, rows * BLK :]] * rows, axis=1), 1.0
    )
    for i in range(per):
        for r in range(rows):
            c_full[me * per + i, r : r + 1, :] = coarse[i : i + 1, r * BLK : (r + 1) * BLK]
    mine_c = c_full.at[pl.ds(me * per, per)]
    to_plane(lambda t: mine_c, mine_c, ca_send, ca_recv)
    transpose_tiles(panel_tiles * 3 // 4, panel_tiles)

    wait_all(halo.at[pl.ds(0, (n_grp - 1) * hr)], halo_recv)
    halo_rhs = jnp.concatenate(
        [
            jnp.concatenate(
                [
                    halo[pl.ds(r * margins + k, n_grp, stride=hr), :]
                    for k in range(margins)
                ],
                axis=1,
            )
            for r in range(rows)
        ],
        axis=0,
    ).astype(BF16)
    inner = jnp.concatenate(
        [
            jnp.concatenate(
                [
                    inner_v[pl.ds(i * deep + r, n_grp, stride=rows), :]
                    for i in range(inner_tiles)
                ],
                axis=1,
            )
            for r in range(rows)
        ],
        axis=0,
    )
    inner = inner + jnp.dot(halo_rhs, wt_v[...], preferred_element_type=F32)
    inner = inner.astype(BF16)

    def scatter_rows(sol, dst, blocks_each):
        for r in range(rows):
            for k in range(blocks_each):
                dst[pl.ds(r * blocks_each + k, n_grp, stride=rows * blocks_each), :] = sol[
                    r * n_grp : (r + 1) * n_grp, k * BLK : (k + 1) * BLK
                ]

    scatter_rows(jnp.dot(inner, w_v[:, width:], preferred_element_type=F32), part_h, margins)
    to_column(
        lambda t: part_h.at[pl.ds(t * hr, hr)], recv_h.at[pl.ds(grp * hr, hr)], h_send, h_recv
    )

    wait_all(c_full.at[pl.ds(0, ncb - per)], ca_recv)
    c_rows = jnp.concatenate([c_full[j] for j in range(ncb)], axis=1).astype(BF16)
    half = v_v.shape[0] // 2
    inner_c = jnp.concatenate(
        [
            jnp.dot(c_rows, vt_v[:, at : at + half], preferred_element_type=F32)
            for at in (0, half)
        ],
        axis=1,
    ).astype(BF16)
    e_mine = jnp.dot(inner_c, v_v[...], preferred_element_type=F32)
    for j in range(ncb):
        e_part[j] = e_mine[:, j * BLK : (j + 1) * BLK]
    to_plane(lambda t: e_part.at[pl.ds(t * per, per)], e_recv.at[me], es_send, es_recv)

    scatter_rows(jnp.dot(inner, w_v[:, :width], preferred_element_type=F32), part_o, own)
    orr = rows * own
    to_column(
        lambda t: part_o.at[pl.ds(t * orr, orr)], recv_o.at[pl.ds(grp * orr, orr)], o_send, o_recv
    )

    wait_all(recv_h.at[pl.ds(0, (n_grp - 1) * hr)], h_recv)
    recv_h[pl.ds(grp * hr, hr)] = part_h[pl.ds(grp * hr, hr)]
    mine_back = back.at[pl.ds(me * hr, hr)]
    back[pl.ds(me * hr, hr)] = jnp.sum(recv_h[...].reshape(n_grp, hr, BLK), axis=0)
    to_plane(lambda t: mine_back, mine_back, back_send, back_recv)

    wait_all(e_recv.at[pl.ds(0, n_sub - 1)], es_recv)
    e_recv[me] = e_part[pl.ds(me * per, per)]
    e_full[pl.ds(me * per, per)] = jnp.sum(e_recv[...], axis=0)
    mine_e = e_full.at[pl.ds(me * per, per)]
    to_plane(lambda t: mine_e, mine_e, ea_send, ea_recv)

    wait_all(recv_o.at[pl.ds(0, (n_grp - 1) * orr)], o_recv)
    recv_o[pl.ds(grp * orr, orr)] = part_o[pl.ds(grp * orr, orr)]
    total = jnp.sum(recv_o[...].reshape(n_grp, orr, BLK), axis=0)
    wait_all(back.at[pl.ds(0, (n_sub - 1) * hr)], back_recv)
    values = jnp.concatenate(
        [
            jnp.concatenate(
                [
                    back[pl.ds(s * hr + r * margins + k, 8, stride=hr), :]
                    for k in range(margins)
                    for s in range(0, n_sub, 8)
                ],
                axis=0,
            )
            for r in range(rows)
        ],
        axis=1,
    )
    returned = split_dot(owner_hot.astype(BF16), values)
    for r in range(rows):
        acc[pl.ds(r, own, stride=rows), :] = (
            total[r * own : (r + 1) * own, :] + returned[:, r * BLK : (r + 1) * BLK]
        )
    load_ids.wait()
    wait_all(e_full.at[pl.ds(0, ncb - per)], ea_recv)
    for b in range(own):
        j = agg_s[0, b]
        at = slice(b * rows, (b + 1) * rows)
        out[at, :] = acc[at, :] + e_full[j]

    wait_all(pick_in.at[pl.ds(0, n_sub - 1)], pick_send)
    wait_all(c_in.at[pl.ds(0, n_sub - 1)], cs_send)
    wait_all(halo.at[pl.ds(0, (n_grp - 1) * hr)], halo_send)
    wait_all(c_full.at[pl.ds(0, ncb - per)], ca_send)
    wait_all(recv_h.at[pl.ds(0, (n_grp - 1) * hr)], h_send)
    wait_all(recv_o.at[pl.ds(0, (n_grp - 1) * orr)], o_send)
    wait_all(e_recv.at[pl.ds(0, n_sub - 1)], es_send)
    wait_all(e_full.at[pl.ds(0, ncb - per)], ea_send)
    wait_all(back.at[pl.ds(0, (n_sub - 1) * hr)], back_send)


def on_device(residual, margin, aggregate, local_factor, coarse_factor):
    n_sub = lax.axis_size("sub")
    n_grp = lax.axis_size("grp")
    rhs, own_width = residual.shape
    own = own_width // BLK
    margins = margin.shape[1]
    inner = local_factor.shape[1]
    ncb = coarse_factor.shape[1] // BLK
    rows = rhs // n_grp
    per = ncb // n_sub
    sizes = (n_sub, n_grp, own, margins, ncb)
    vm = pltpu.VMEM
    sem = pltpu.SemaphoreType.DMA
    result = pl.pallas_call(
        functools.partial(kernel, sizes),
        out_shape=pltpu.VMEM((rows * own, BLK), F32),
        in_specs=[
            pl.BlockSpec(memory_space=pl.ANY),
            pl.BlockSpec(memory_space=pl.ANY),
            pl.BlockSpec(memory_space=pl.ANY),
            pl.BlockSpec(memory_space=pl.ANY),
            pl.BlockSpec(memory_space=pl.ANY),
        ],
        out_specs=pl.BlockSpec(memory_space=pltpu.VMEM),
        scratch_shapes=[
            vm((margins, n_sub), jnp.int32),
            vm((1, own), jnp.int32),
            pltpu.SMEM((1, own), jnp.int32),
            vm((own * rhs, BLK), F32),
            vm((inner, own_width + margins * BLK), BF16),
            vm(coarse_factor.shape, BF16),
            vm(coarse_factor.shape[::-1], BF16),
            vm((margins * BLK, inner), BF16),
            vm((rows * own, BLK), F32),
            vm((n_sub * rows * margins, BLK), F32),
            vm((n_sub, rows * margins, BLK), F32),
            vm((n_sub, per, (rows + 1) * BLK), F32),
            vm((n_sub, per, (rows + 1) * BLK), F32),
            vm((ncb, rows, BLK), F32),
            vm((n_grp * rows * margins, BLK), F32),
            vm((rhs * inner // BLK, BLK), F32),
            vm((n_grp * rows * margins, BLK), F32),
            vm((n_grp * rows * margins, BLK), F32),
            vm((n_grp * rows * own, BLK), F32),
            vm((n_grp * rows * own, BLK), F32),
            vm((n_sub * rows * margins, BLK), F32),
            vm((ncb, rows, BLK), F32),
            vm((n_sub, per, rows, BLK), F32),
            vm((ncb, rows, BLK), F32),
            vm((rows * own, BLK), F32),
            sem((6,)),
        ] + [sem] * 18,
        compiler_params=pltpu.CompilerParams(collective_id=0, has_side_effects=True),
    )(margin.T, aggregate.reshape(1, own), residual, local_factor, coarse_factor)
    return result.reshape(own, rows, BLK).transpose(1, 0, 2).reshape(rows, own_width)


def solution(mesh):
    placed = (P(None, "sub"), P(), P("sub"), P("sub", "grp", None), P("sub", None))
    return jax.shard_map(
        on_device, mesh=mesh, in_specs=placed, out_specs=P("grp", "sub"), check_vma=False
    )
```

```python
import functools

import jax
import jax.numpy as jnp
from jax import lax
from jax.experimental import pallas as pl
from jax.experimental.pallas import tpu as pltpu
from jax.sharding import PartitionSpec as P

BLK = 128
F32 = jnp.float32
BF16 = jnp.bfloat16
MESH = pl.DeviceIdType.MESH
NT = (((1,), (1,)), ((), ()))
TN = (((0,), (0,)), ((), ()))


def split(values):
    high = values.astype(BF16)
    return high, (values - high.astype(F32)).astype(BF16)


def split_dot(onehot, values):
    high, low = split(values)
    return jnp.dot(onehot, high, preferred_element_type=F32) + jnp.dot(
        onehot, low, preferred_element_type=F32
    )


def wait_all(ref, sem):
    pltpu.make_async_copy(ref, ref, sem).wait()


def kernel(
    sizes,
    margin, aggregate, residual, local_factor, coarse_factor,
    out,
    margin_v, agg_v, agg_s, res_v, w_v, v_v, vt_v, wt_v, mine, pick_out, pick_in, c_out, c_in, c_full, halo, inner_v,
    part_h, recv_h, part_o, recv_o, back, e_part, e_recv, e_full, acc,
    load_sem, pick_send, pick_recv, cs_send, cs_recv, ca_send, ca_recv, halo_send, halo_recv,
    h_send, h_recv, o_send, o_recv, back_send, back_recv, es_send, es_recv, ea_send, ea_recv,
):
    n_sub, n_grp, own, margins, ncb = sizes
    rows = 2
    per = ncb // n_sub
    me = lax.axis_index("sub")
    grp = lax.axis_index("grp")

    barrier = pltpu.get_barrier_semaphore()

    ny = 4
    nx = n_sub // (2 * ny)
    x = lax.div(me, 2 * ny)
    y = lax.rem(lax.div(me, 2), ny)
    core = lax.rem(me, 2)

    def far(d, n):
        return min(d, n - d)

    steps = [(dx, dy, dc) for dx in range(nx) for dy in range(ny) for dc in range(2)]
    steps = sorted(steps[1:], key=lambda t: -far(t[0], nx) - far(t[1], ny))
    xs = [lax.rem(x + d, nx) * (2 * ny) for d in range(nx)]
    ys = [lax.rem(y + d, ny) * 2 for d in range(ny)]
    cores = [core, 1 - core]
    plane = [(grp, xs[dx] + ys[dy] + cores[dc]) for dx, dy, dc in steps]
    column = [
        (lax.rem(grp + d, n_grp), me) for d in sorted(range(1, n_grp), key=lambda d: -far(d, n_grp))
    ]
    far_z = [far(d, n_grp) for d in sorted(range(1, n_grp), key=lambda d: -far(d, n_grp))]
    far_p = [far(dx, nx) + far(dy, ny) for dx, dy, _ in steps]
    ranked = sorted(zip(far_z + far_p, range(len(far_z + far_p))), key=lambda t: -t[0])
    for target in [(column + plane)[i] for _, i in ranked]:
        pl.semaphore_signal(barrier, inc=1, device_id=target, device_id_type=MESH)

    load_margin = pltpu.make_async_copy(margin, margin_v, load_sem.at[3])
    load_agg = pltpu.make_async_copy(aggregate, agg_v, load_sem.at[4])
    load_ids = pltpu.make_async_copy(aggregate, agg_s, load_sem.at[5])
    load_margin.start()
    load_agg.start()
    load_ids.start()
    for b in range(own):
        pltpu.make_async_copy(
            residual.at[:, pl.ds(b * BLK, BLK)],
            res_v.at[pl.ds(b * rows * n_grp, rows * n_grp)],
            load_sem.at[0],
        ).start()
    load_w = pltpu.make_async_copy(local_factor.at[0], w_v, load_sem.at[1])
    load_v = pltpu.make_async_copy(coarse_factor, v_v, load_sem.at[2])
    load_w.start()
    load_v.start()

    def to_plane(src, dst, send, recv):
        for target in plane:
            pltpu.make_async_remote_copy(
                src_ref=src(target[1]), dst_ref=dst, send_sem=send, recv_sem=recv,
                device_id=target, device_id_type=MESH,
            ).start()

    def to_column(src, dst, send, recv):
        for target in column:
            pltpu.make_async_remote_copy(
                src_ref=src(target[0]), dst_ref=dst, send_sem=send, recv_sem=recv,
                device_id=target, device_id_type=MESH,
            ).start()

    slots = n_sub * margins
    each = BLK // n_sub
    lane = lax.broadcasted_iota(jnp.int32, (1, BLK), 1)
    own_ids = lax.broadcasted_iota(jnp.int32, (own, BLK), 0) + me * own
    load_margin.wait()
    spread = jnp.concatenate([margin_v[...]] * each, axis=1)
    tables = []
    for first in range(0, margins, each):
        row = jnp.full((1, BLK), -1, jnp.int32)
        for i in range(min(each, margins - first)):
            here = jnp.logical_and(lane >= i * n_sub, lane < (i + 1) * n_sub)
            row = jnp.where(here, spread[first + i : first + i + 1, :], row)
        tables.append((jnp.broadcast_to(row, (own, BLK)) == own_ids).astype(F32))
    owner_hot = jnp.concatenate(tables, axis=1)[:, :slots]
    load_agg.wait()
    coarse_hot = (
        jnp.broadcast_to(agg_v[...], (ncb, own)) == lax.broadcasted_iota(jnp.int32, (ncb, own), 0)
    ).astype(F32)

    wait_all(res_v, load_sem.at[0])
    for b in range(own):
        for r in range(rows):
            mine[r * own + b : r * own + b + 1, :] = res_v[
                pl.ds(b * rows * n_grp + grp * rows + r, 1), :
            ]
    blocks = jnp.concatenate([mine[r * own : (r + 1) * own, :] for r in range(rows)], axis=1)
    high, low = split(blocks)
    picked = lax.dot_general(owner_hot.astype(BF16), high, TN, preferred_element_type=F32)
    hr = rows * margins
    for r in range(rows):
        for k in range(margins):
            for t in range(0, n_sub, 8):
                at = k * n_sub + t
                pick_out[pl.ds(t * hr + r * margins + k, 8, stride=hr), :] = picked[
                    at : at + 8, r * BLK : (r + 1) * BLK
                ]
    hot = coarse_hot.astype(BF16)
    sums = jnp.dot(hot, high, preferred_element_type=F32) + jnp.dot(
        hot, low, preferred_element_type=F32
    )
    count = jnp.broadcast_to(jnp.sum(coarse_hot, axis=1, keepdims=True), (ncb, BLK))
    sums = jnp.concatenate([sums, count], axis=1)
    for t in range(n_sub):
        c_out[t] = sums[t * per : (t + 1) * per, :]

    pl.semaphore_wait(barrier, n_sub - 1 + n_grp - 1)
    to_plane(lambda t: pick_out.at[pl.ds(t * hr, hr)], pick_in.at[me], pick_send, pick_recv)
    to_plane(lambda t: c_out.at[t], c_in.at[me], cs_send, cs_recv)

    load_w.wait()
    width = own * BLK
    deep = rows * n_grp
    inner = lax.dot_general(
        jnp.concatenate(
            [res_v[b * deep : (b + 1) * deep, :].astype(BF16) for b in range(own)], axis=1
        ),
        w_v[:, :width], NT, preferred_element_type=F32,
    )
    inner_tiles = inner.shape[1] // BLK
    for i in range(inner_tiles):
        inner_v[i * deep : (i + 1) * deep, :] = inner[:, i * BLK : (i + 1) * BLK]

    for k in range(0, margins, 2):
        at = k * BLK
        wt_v[at : at + 2 * BLK, :] = w_v[:, width + at : width + at + 2 * BLK].T

    load_v.wait()
    tile = 2 * BLK
    panel_tiles = v_v.shape[1] // tile

    def transpose_tiles(begin, end):
        def one(n, carry):
            at = pl.ds(pl.multiple_of(n * tile, tile), tile)
            vt_v[at, :] = v_v[:, at].T
            return carry

        lax.fori_loop(begin, end, one, 0)

    transpose_tiles(0, panel_tiles // 2)

    wait_all(pick_in.at[pl.ds(0, n_sub - 1)], pick_recv)
    pick_in[me] = jnp.zeros((hr, BLK), F32)
    halo[pl.ds(grp * hr, hr)] = jnp.sum(pick_in[...], axis=0)
    mine_halo = halo.at[pl.ds(grp * hr, hr)]
    to_column(lambda t: mine_halo, mine_halo, halo_send, halo_recv)

    wait_all(c_in.at[pl.ds(0, n_sub - 1)], cs_recv)
    c_in[me] = c_out[me]
    sums = jnp.sum(c_in[...], axis=0)
    coarse = sums[:, : rows * BLK] / jnp.maximum(
        jnp.concatenate([sums[:, rows * BLK :]] * rows, axis=1), 1.0
    )
    for i in range(per):
        for r in range(rows):
            c_full[me * per + i, r : r + 1, :] = coarse[i : i + 1, r * BLK : (r + 1) * BLK]
    mine_c = c_full.at[pl.ds(me * per, per)]
    to_plane(lambda t: mine_c, mine_c, ca_send, ca_recv)
    transpose_tiles(panel_tiles // 2, panel_tiles)

    wait_all(halo.at[pl.ds(0, (n_grp - 1) * hr)], halo_recv)
    halo_rhs = jnp.concatenate(
        [
            jnp.concatenate(
                [
                    halo[pl.ds(r * margins + k, n_grp, stride=hr), :]
                    for k in range(margins)
                ],
                axis=1,
            )
            for r in range(rows)
        ],
        axis=0,
    ).astype(BF16)
    inner = jnp.concatenate(
        [
            jnp.concatenate(
                [
                    inner_v[pl.ds(i * deep + r, n_grp, stride=rows), :]
                    for i in range(inner_tiles)
                ],
                axis=1,
            )
            for r in range(rows)
        ],
        axis=0,
    )
    inner = inner + jnp.dot(halo_rhs, wt_v[...], preferred_element_type=F32)
    inner = inner.astype(BF16)

    def scatter_rows(sol, dst, blocks_each):
        for r in range(rows):
            for k in range(blocks_each):
                dst[pl.ds(r * blocks_each + k, n_grp, stride=rows * blocks_each), :] = sol[
                    r * n_grp : (r + 1) * n_grp, k * BLK : (k + 1) * BLK
                ]

    scatter_rows(jnp.dot(inner, w_v[:, width:], preferred_element_type=F32), part_h, margins)
    to_column(
        lambda t: part_h.at[pl.ds(t * hr, hr)], recv_h.at[pl.ds(grp * hr, hr)], h_send, h_recv
    )

    wait_all(c_full.at[pl.ds(0, ncb - per)], ca_recv)
    c_rows = jnp.concatenate([c_full[j] for j in range(ncb)], axis=1).astype(BF16)
    half = v_v.shape[0] // 2
    inner_c = jnp.concatenate(
        [
            jnp.dot(c_rows, vt_v[:, at : at + half], preferred_element_type=F32)
            for at in (0, half)
        ],
        axis=1,
    ).astype(BF16)
    e_mine = jnp.dot(inner_c, v_v[...], preferred_element_type=F32)
    for j in range(ncb):
        e_part[j] = e_mine[:, j * BLK : (j + 1) * BLK]
    to_plane(lambda t: e_part.at[pl.ds(t * per, per)], e_recv.at[me], es_send, es_recv)

    wait_all(recv_h.at[pl.ds(0, (n_grp - 1) * hr)], h_recv)
    recv_h[pl.ds(grp * hr, hr)] = part_h[pl.ds(grp * hr, hr)]
    mine_back = back.at[pl.ds(me * hr, hr)]
    back[pl.ds(me * hr, hr)] = jnp.sum(recv_h[...].reshape(n_grp, hr, BLK), axis=0)
    to_plane(lambda t: mine_back, mine_back, back_send, back_recv)

    scatter_rows(jnp.dot(inner, w_v[:, :width], preferred_element_type=F32), part_o, own)
    orr = rows * own
    to_column(
        lambda t: part_o.at[pl.ds(t * orr, orr)], recv_o.at[pl.ds(grp * orr, orr)], o_send, o_recv
    )

    wait_all(e_recv.at[pl.ds(0, n_sub - 1)], es_recv)
    e_recv[me] = e_part[pl.ds(me * per, per)]
    e_full[pl.ds(me * per, per)] = jnp.sum(e_recv[...], axis=0)
    mine_e = e_full.at[pl.ds(me * per, per)]
    to_plane(lambda t: mine_e, mine_e, ea_send, ea_recv)

    wait_all(recv_o.at[pl.ds(0, (n_grp - 1) * orr)], o_recv)
    recv_o[pl.ds(grp * orr, orr)] = part_o[pl.ds(grp * orr, orr)]
    total = jnp.sum(recv_o[...].reshape(n_grp, orr, BLK), axis=0)
    wait_all(back.at[pl.ds(0, (n_sub - 1) * hr)], back_recv)
    values = jnp.concatenate(
        [
            jnp.concatenate(
                [
                    back[pl.ds(s * hr + r * margins + k, 8, stride=hr), :]
                    for k in range(margins)
                    for s in range(0, n_sub, 8)
                ],
                axis=0,
            )
            for r in range(rows)
        ],
        axis=1,
    )
    returned = split_dot(owner_hot.astype(BF16), values)
    for r in range(rows):
        acc[pl.ds(r, own, stride=rows), :] = (
            total[r * own : (r + 1) * own, :] + returned[:, r * BLK : (r + 1) * BLK]
        )
    load_ids.wait()
    wait_all(e_full.at[pl.ds(0, ncb - per)], ea_recv)
    for b in range(own):
        j = agg_s[0, b]
        at = slice(b * rows, (b + 1) * rows)
        out[at, :] = acc[at, :] + e_full[j]

    wait_all(pick_in.at[pl.ds(0, n_sub - 1)], pick_send)
    wait_all(c_in.at[pl.ds(0, n_sub - 1)], cs_send)
    wait_all(halo.at[pl.ds(0, (n_grp - 1) * hr)], halo_send)
    wait_all(c_full.at[pl.ds(0, ncb - per)], ca_send)
    wait_all(recv_h.at[pl.ds(0, (n_grp - 1) * hr)], h_send)
    wait_all(recv_o.at[pl.ds(0, (n_grp - 1) * orr)], o_send)
    wait_all(e_recv.at[pl.ds(0, n_sub - 1)], es_send)
    wait_all(e_full.at[pl.ds(0, ncb - per)], ea_send)
    wait_all(back.at[pl.ds(0, (n_sub - 1) * hr)], back_send)


def on_device(residual, margin, aggregate, local_factor, coarse_factor):
    n_sub = lax.axis_size("sub")
    n_grp = lax.axis_size("grp")
    rhs, own_width = residual.shape
    own = own_width // BLK
    margins = margin.shape[1]
    inner = local_factor.shape[1]
    ncb = coarse_factor.shape[1] // BLK
    rows = rhs // n_grp
    per = ncb // n_sub
    sizes = (n_sub, n_grp, own, margins, ncb)
    vm = pltpu.VMEM
    sem = pltpu.SemaphoreType.DMA
    result = pl.pallas_call(
        functools.partial(kernel, sizes),
        out_shape=pltpu.VMEM((rows * own, BLK), F32),
        in_specs=[
            pl.BlockSpec(memory_space=pl.ANY),
            pl.BlockSpec(memory_space=pl.ANY),
            pl.BlockSpec(memory_space=pl.ANY),
            pl.BlockSpec(memory_space=pl.ANY),
            pl.BlockSpec(memory_space=pl.ANY),
        ],
        out_specs=pl.BlockSpec(memory_space=pltpu.VMEM),
        scratch_shapes=[
            vm((margins, n_sub), jnp.int32),
            vm((1, own), jnp.int32),
            pltpu.SMEM((1, own), jnp.int32),
            vm((own * rhs, BLK), F32),
            vm((inner, own_width + margins * BLK), BF16),
            vm(coarse_factor.shape, BF16),
            vm(coarse_factor.shape[::-1], BF16),
            vm((margins * BLK, inner), BF16),
            vm((rows * own, BLK), F32),
            vm((n_sub * rows * margins, BLK), F32),
            vm((n_sub, rows * margins, BLK), F32),
            vm((n_sub, per, (rows + 1) * BLK), F32),
            vm((n_sub, per, (rows + 1) * BLK), F32),
            vm((ncb, rows, BLK), F32),
            vm((n_grp * rows * margins, BLK), F32),
            vm((rhs * inner // BLK, BLK), F32),
            vm((n_grp * rows * margins, BLK), F32),
            vm((n_grp * rows * margins, BLK), F32),
            vm((n_grp * rows * own, BLK), F32),
            vm((n_grp * rows * own, BLK), F32),
            vm((n_sub * rows * margins, BLK), F32),
            vm((ncb, rows, BLK), F32),
            vm((n_sub, per, rows, BLK), F32),
            vm((ncb, rows, BLK), F32),
            vm((rows * own, BLK), F32),
            sem((6,)),
        ] + [sem] * 18,
        compiler_params=pltpu.CompilerParams(collective_id=0, has_side_effects=True),
    )(margin.T, aggregate.reshape(1, own), residual, local_factor, coarse_factor)
    return result.reshape(own, rows, BLK).transpose(1, 0, 2).reshape(rows, own_width)


def solution(mesh):
    placed = (P(None, "sub"), P(), P("sub"), P("sub", "grp", None), P("sub", None))
    return jax.shard_map(
        on_device, mesh=mesh, in_specs=placed, out_specs=P("grp", "sub"), check_vma=False
    )
```
